256 devices in a mesh: space: 16 (over z, core), mode: 16 (over y, x).
Axes of the slice: x: 4, y: 4, z: 8, core: 2. Of those that a mesh axis runs over, the one named last changes fastest.
Arguments:
- guess: float32 [8192, 2048], P('space', 'mode'), may hold values from -6 to 6
- forcing: float32 [8192, 2048], P('space', 'mode'), may hold values from -6 to 6
- spatial_diag: bfloat16 [8192, 512], P('space'), may hold values from -0.25 to 0.25
- spatial_ghost: bfloat16 [8192, 256], P('space'), may hold values from -0.375 to 0.375
- ghost_rows: int32 [32, 128], P('space'), may hold values from 0 to 511, as said below
- chaos_vals: bfloat16 [128, 128, 128], P('mode'), may hold values from -0.25 to 0.25
- chaos_targets: int32 [16, 8], replicated, may hold values from 0 to 15, as said below
- chaos_count: int32 [16], replicated, may hold values from 1 to 8, as said below
- mean_inverse: bfloat16 [2048, 2048], replicated, may hold values from -0.125 to 0.125
Outputs:
- field: float32 [8192, 2048], P('space', 'mode')
The draws below stay inside these ranges and needn't reach their ends.
Inputs may be any that keep to these rules, and one draw needn't show every extreme that they name: `ghost_rows`: each row holds 128 distinct node numbers, 0 and 511 among them. `chaos_targets`: the targets in a row are distinct and the first is the row's own chaos block. Only the first chaos_count[j] slots of row j are used; some row uses all 8 slots and some row only one.
All inputs are finite; a program needn't handle non-finite values.
Results may differ from the reference program's by a relative error of at most 0.0021.
Values may be sent and summed in bfloat16 or wider, within the bound.
A program may use at most 128 MiB of HBM per device.

```python
import jax
import jax.numpy as jnp
from jax import lax

NODE_DEV = 512
GHOST = 128
MODES = 2048
CB = 128
LIST = 8
ITERS = 3
NODES = 8192


def chaos_lists(key):
    mode_blocks = MODES // CB
    base = jax.random.fold_in(key, 71)
    keys = jax.random.split(base, mode_blocks + 3)

    def offsets_for(sub_key):
        return jax.random.permutation(sub_key, mode_blocks - 1)[:LIST - 1].astype(jnp.int32) + 1
    offsets = jax.vmap(offsets_for)(keys[:mode_blocks])
    own = jnp.arange(mode_blocks, dtype=jnp.int32)[:, None]
    steps_away = jnp.concatenate([jnp.zeros((mode_blocks, 1), jnp.int32), offsets], axis=1)
    targets = (own + steps_away) % mode_blocks
    first_draw = jax.random.randint(keys[mode_blocks], (mode_blocks,), 1, LIST + 1)
    second_draw = jax.random.randint(keys[mode_blocks + 1], (mode_blocks,), 1, LIST + 1)
    counts = jnp.minimum(first_draw, second_draw).astype(jnp.int32)
    fullest = jax.random.randint(keys[mode_blocks + 2], (), 0, mode_blocks)
    counts = counts.at[fullest].set(LIST)
    counts = counts.at[(fullest + 1) % mode_blocks].set(1)
    return (targets.astype(jnp.int32), counts.astype(jnp.int32))


def draw_chaos_targets(key, part):
    return chaos_lists(key)[0]


def draw_chaos_count(key, part):
    return chaos_lists(key)[1]


def draw_ghost_rows(key, part):
    list_count = 2 * (NODES // NODE_DEV)
    keys = jax.random.split(jax.random.fold_in(key, 13), list_count)

    def one_list(sub_key):
        first_key, second_key = jax.random.split(sub_key)
        inner = jax.random.permutation(first_key, NODE_DEV - 2)[:GHOST - 2].astype(jnp.int32) + 1
        chosen = jnp.concatenate([jnp.array([0, NODE_DEV - 1], jnp.int32), inner])
        return chosen[jax.random.permutation(second_key, GHOST)]
    return jax.vmap(one_list)(keys).astype(jnp.int32)


def shard_levels(stream_key, shape, pieces, least, largest):
    def one(axis_at, parts):
        heights = jax.random.uniform(jax.random.fold_in(jax.random.fold_in(stream_key, 6), axis_at), (parts,), jnp.float32, least / len(pieces), largest / len(pieces))
        return jnp.repeat(jnp.exp(heights), shape[axis_at] // parts).reshape((-1,) + (1,) * (len(shape) - axis_at - 1))

    level = one(*pieces[0])
    for cut in pieces[1:]:
        level = level * one(*cut)
    return level


def centred(key, shape, spread, limit, cuts=(), kind=jnp.bfloat16):
    entries = jax.random.normal(key, shape, jnp.float32) * spread
    if len(cuts) > 0:
        entries = shard_levels(key, shape, cuts, -0.22, 0.18) * entries
    return jnp.clip(entries, min=-limit, max=limit).astype(kind)


def setup_inputs(seed: int = 0) -> dict:
    key_of = jax.random.split(jax.random.key(seed), 10)
    return {
        "guess": centred(key_of[0], (NODES, MODES), 1.0, 6.0, ((0, 16), (1, 16)), jnp.float32),
        "forcing": centred(key_of[1], (NODES, MODES), 1.0, 6.0, ((0, 16), (1, 16)), jnp.float32),
        "spatial_diag": centred(key_of[2], (NODES, NODE_DEV), NODE_DEV ** -0.5, 0.25, ((0, 16),)),
        "spatial_ghost": centred(key_of[3], (NODES, 2 * GHOST), (2 * GHOST) ** -0.5, 0.375, ((0, 16),)),
        "ghost_rows": draw_ghost_rows(jax.random.fold_in(key_of[9], 71), 0),
        "chaos_vals": centred(key_of[5], (MODES // CB * LIST, CB, CB), (4 * CB) ** -0.5, 0.25, ((0, 16),)),
        "chaos_targets": draw_chaos_targets(jax.random.fold_in(key_of[9], 71), 0),
        "chaos_count": draw_chaos_count(jax.random.fold_in(key_of[9], 71), 0),
        "mean_inverse": centred(key_of[8], (MODES, MODES), MODES ** -0.5, 0.125),
    }


step_gain = 0.5

def reference(guess, forcing, spatial_diag, spatial_ghost, ghost_rows, chaos_vals, chaos_targets, chaos_count, mean_inverse):
    space_blocks = NODES // NODE_DEV
    mode_blocks = MODES // CB
    indices = ghost_rows.reshape(space_blocks, 2, GHOST).astype(jnp.int32)
    diag_full = spatial_diag.astype(jnp.float32).reshape(space_blocks, NODE_DEV, NODE_DEV)
    ghost_full = spatial_ghost.astype(jnp.float32).reshape(space_blocks, NODE_DEV, 2 * GHOST)
    inverse_full = mean_inverse.astype(jnp.float32)
    values_full = chaos_vals.astype(jnp.float32).reshape(mode_blocks, LIST, CB, CB)
    field = guess
    for iteration in range(ITERS):
        field_low = lax.optimization_barrier(field.astype(jnp.bfloat16)).astype(jnp.float32)
        blocks = field_low.reshape(space_blocks, NODE_DEV, MODES)
        lower_sent = jnp.take_along_axis(blocks, indices[:, 0, :, None], axis=1)
        upper_sent = jnp.take_along_axis(blocks, indices[:, 1, :, None], axis=1)
        empty = jnp.zeros((1, GHOST, MODES), jnp.float32)
        from_below = jnp.concatenate([empty, upper_sent[:-1]], axis=0)
        from_above = jnp.concatenate([lower_sent[1:], empty], axis=0)
        ghosts = jnp.concatenate([from_below, from_above], axis=1)
        spatial = jnp.einsum('bij,bjm->bim', diag_full, blocks, precision=lax.Precision.HIGHEST)
        spatial = spatial + jnp.einsum('bij,bjm->bim', ghost_full, ghosts, precision=lax.Precision.HIGHEST)
        spatial = spatial.reshape(NODES, MODES)
        columns = field_low.reshape(NODES, mode_blocks, CB)

        def add_pair(pair, coupled):
            pair = jnp.asarray(pair).astype(jnp.int32)
            source_block = pair // LIST
            slot = pair % LIST
            target = chaos_targets[source_block, slot].astype(jnp.int32)
            active = (slot < chaos_count[source_block]).astype(jnp.float32)
            source = lax.dynamic_index_in_dim(columns, source_block, 1, keepdims=False)
            product = jnp.dot(source, values_full[source_block, slot].T, precision=lax.Precision.HIGHEST) * active
            current = lax.dynamic_index_in_dim(coupled, target, 1, keepdims=False)
            return lax.dynamic_update_index_in_dim(coupled, current + product, target, 1)
        coupled = lax.fori_loop(0, mode_blocks * LIST, add_pair, jnp.zeros((NODES, mode_blocks, CB), jnp.float32))
        residual = forcing - spatial - coupled.reshape(NODES, MODES)
        residual_low = lax.optimization_barrier(residual.astype(jnp.bfloat16)).astype(jnp.float32)
        update = jnp.dot(residual_low, inverse_full.T, precision=lax.Precision.HIGHEST)
        damping = step_gain / jnp.sqrt(jnp.mean(update * update) + 1e-06)
        field = field + damping * update
    return field
```

```python
import functools

import jax
import jax.numpy as jnp
from jax import lax
from jax.experimental import pallas as pl
from jax.experimental.pallas import tpu as pltpu
from jax.sharding import PartitionSpec as P

STEPS = 3
step_gain = 0.5
BF = jnp.bfloat16
F32 = jnp.float32
A_F, A_SF, A_G, A_GLO, A_SG, A_S2F, A_S2G = range(7)
PLACE = {A_F: (0, 0), A_SF: (0, 1), A_S2F: (0, 2), A_G: (1, 0), A_SG: (1, 1), A_S2G: (1, 2), A_GLO: (1, 3)}


def dot(a, b):
    return jnp.dot(a, b, preferred_element_type=F32)


def split(x):
    high = x.astype(BF)
    return high, (x - high.astype(F32)).astype(BF)


def kernel(
    sizes,
    f_ref, force_ref, sd_ref, sg_ref, rows_ref, vals_ref, inv_ref, m_hbm,
    o_ref,
    m_ref, c_ref, cv_ref, oh_ref, arr_ref, gsend_ref, ghost_ref,
    got_ref, x_ref, add_ref, v_ref, back_src, back_got, gram_src, gram_got,
    m_sem, l_sem, gh_send, gh_recv, a_send, a_recv, c_send, c_recv, b_send, b_recv, r_send, r_recv,
):
    ns, nm, nx, slab, ghost, width, slots = sizes
    ny = nm // nx
    half = slots // 2
    nodes = f_ref.shape[0]
    s, m = lax.axis_index("space"), lax.axis_index("mode")
    c = s % 2
    y, x = m // nx, m % nx
    mesh = pl.DeviceIdType.MESH

    def send(src, dst, ssem, rsem, to_s, to_m):
        cp = pltpu.make_async_remote_copy(
            src_ref=src, dst_ref=dst, send_sem=ssem, recv_sem=rsem,
            device_id={"space": to_s, "mode": to_m}, device_id_type=mesh,
        )
        cp.start()

    def arrived(dst, rsem):
        pltpu.make_async_remote_copy(
            src_ref=dst, dst_ref=dst, send_sem=rsem, recv_sem=rsem,
            device_id={"space": s, "mode": m}, device_id_type=mesh,
        ).wait_recv()

    def sent(src, ssem):
        pltpu.make_async_remote_copy(
            src_ref=src, dst_ref=src, send_sem=ssem, recv_sem=ssem,
            device_id={"space": s, "mode": m}, device_id_type=mesh,
        ).wait_send()

    barrier = pltpu.get_barrier_semaphore()

    def greet_mode(k, _):
        pl.semaphore_signal(barrier, inc=1, device_id={"space": s, "mode": (m + k) % nm}, device_id_type=mesh)
        return 0

    def greet_space(k, _):
        pl.semaphore_signal(barrier, inc=1, device_id={"space": (s + k) % ns, "mode": m}, device_id_type=mesh)
        return 0

    lax.fori_loop(1, nm, greet_mode, 0)
    lax.fori_loop(1, ns, greet_space, 0)

    m_copy = pltpu.make_async_copy(m_hbm, m_ref, m_sem)
    m_copy.start()
    own_copy = pltpu.make_async_copy(vals_ref, cv_ref.at[m, pl.ds(0, slots)], l_sem)
    own_copy.start()

    f_bf = f_ref[...].astype(BF)
    arr_ref[A_F] = f_bf
    for side in range(2):
        hits = lax.broadcasted_iota(jnp.int32, (nodes, ghost), 0) == rows_ref[side : side + 1, :]
        picks = jnp.transpose(jnp.where(hits, 1.0, 0.0).astype(F32))
        oh_ref[side * ghost : (side + 1) * ghost, :] = picks.astype(BF)
    picked = dot(oh_ref[...], f_bf).astype(BF)
    gsend_ref[0, :, 0:width] = picked

    def zero_tail(j, _):
        cv_ref[j, slots] = jnp.zeros((width, width), BF)
        got_ref[0, j, pl.ds(3 * slab, slab), :] = jnp.zeros((slab, width), BF)
        return 0

    lax.fori_loop(0, nm, zero_tail, 0)

    @pl.when(s == 0)
    def _():
        for r in range(3):
            ghost_ref[r, 0:ghost, :] = jnp.zeros((ghost, 2 * width), BF)

    @pl.when(s == ns - 1)
    def _():
        for r in range(3):
            ghost_ref[r, ghost : 2 * ghost, :] = jnp.zeros((ghost, 2 * width), BF)

    pl.semaphore_wait(barrier, nm - 1 + ns - 1)

    wide = [width, 2 * width, width]

    def ghosts_out(r):
        w = wide[r]

        @pl.when(s > 0)
        def _():
            send(gsend_ref.at[r, pl.ds(0, ghost), pl.ds(0, w)], ghost_ref.at[r, pl.ds(ghost, ghost), pl.ds(0, w)],
                 gh_send.at[r, 0], gh_recv.at[r, 1], s - 1, m)

        @pl.when(s < ns - 1)
        def _():
            send(gsend_ref.at[r, pl.ds(ghost, ghost), pl.ds(0, w)], ghost_ref.at[r, pl.ds(0, ghost), pl.ds(0, w)],
                 gh_send.at[r, 1], gh_recv.at[r, 0], s + 1, m)

    def ghosts_in(r):
        w = wide[r]

        @pl.when(s > 0)
        def _():
            arrived(ghost_ref.at[r, pl.ds(0, ghost), pl.ds(0, w)], gh_recv.at[r, 0])

        @pl.when(s < ns - 1)
        def _():
            arrived(ghost_ref.at[r, pl.ds(ghost, ghost), pl.ds(0, w)], gh_recv.at[r, 1])

    def ghosts_sent(r):
        w = wide[r]

        @pl.when(s > 0)
        def _():
            sent(gsend_ref.at[r, pl.ds(0, ghost), pl.ds(0, w)], gh_send.at[r, 0])

        @pl.when(s < ns - 1)
        def _():
            sent(gsend_ref.at[r, pl.ds(ghost, ghost), pl.ds(0, w)], gh_send.at[r, 1])

    def spread(a):
        buf, row = PLACE[a]

        def one(k, _):
            to = (m + k) % nm
            send(arr_ref.at[a, pl.ds(to * slab, slab), :], got_ref.at[buf, m, pl.ds(row * slab, slab), :],
                 a_send.at[a, to], a_recv.at[a, m], s, to)
            return 0

        lax.fori_loop(1, nm, one, 0)
        got_ref[buf, m, pl.ds(row * slab, slab), :] = arr_ref[a, pl.ds(m * slab, slab), :]

    def first_axis(k):
        return ((y + k * c) % ny) * nx + (x + k * (1 - c)) % nx

    def moved(j, k):
        jy, jx = j // nx, j % nx
        return ((jy + k * (1 - c)) % ny) * nx + (jx + k * c) % nx

    mine = pl.ds(c * half, half)
    partner = s + 1 - 2 * c

    def table(j, h):
        return cv_ref.at[j, pl.ds(h * half, half)]

    def first_leg():
        for k in range(1, nx):
            send(vals_ref.at[mine], table(m, c), c_send.at[k - 1], c_recv.at[m, c], s, first_axis(k))
        for k in range(1, nx):
            send(vals_ref.at[mine], table(m, c), c_send.at[nx - 1 + k - 1], c_recv.at[m, c], s, moved(m, k))

    def second_leg():
        for k in range(1, nx):
            j = first_axis(nx - k)
            arrived(table(j, c), c_recv.at[j, c])
            for q in range(1, nx):
                send(table(j, c), table(j, c), c_send.at[(k + 1) * (nx - 1) + q - 1], c_recv.at[j, c], s, moved(m, q))
            send(table(j, c), table(j, c), c_send.at[nx * nx - 1 + j], c_recv.at[j, c], partner, m)

    def last_leg():
        for k in range(nx):
            for q in range(1, nx):
                j = moved(first_axis((nx - k) % nx), nx - q)
                arrived(table(j, c), c_recv.at[j, c])
                send(table(j, c), table(j, c), c_send.at[nx * nx - 1 + j], c_recv.at[j, c], partner, m)
        for k in range(1, nm):
            j = (m + k) % nm
            arrived(table(j, 1 - c), c_recv.at[j, 1 - c])

    ghosts_out(0)
    first_leg()
    spread(A_F)
    part = dot(sd_ref[...], f_bf)
    ghosts_in(0)
    sf = part + dot(sg_ref[...], ghost_ref[0, :, 0:width])
    g_high, g_low = split(force_ref[...] - sf)
    sf_bf = sf.astype(BF)
    both = jnp.concatenate([g_high, sf_bf], axis=1)
    gsend_ref[1] = dot(oh_ref[...], both).astype(BF)
    ghosts_out(1)
    arr_ref[A_SF] = sf_bf
    arr_ref[A_G] = g_high
    arr_ref[A_GLO] = g_low
    spread(A_SF)
    spread(A_G)
    spread(A_GLO)
    part = dot(sd_ref[...], both)
    ghosts_in(1)
    two = (part + dot(sg_ref[...], ghost_ref[1])).astype(BF)
    sg_bf = two[:, 0:width]
    gsend_ref[2, :, 0:width] = dot(oh_ref[...], sg_bf).astype(BF)
    ghosts_out(2)
    arr_ref[A_SG] = sg_bf
    arr_ref[A_S2F] = two[:, width : 2 * width]
    spread(A_SG)
    spread(A_S2F)
    second_leg()
    part = dot(sd_ref[...], sg_bf)
    ghosts_in(2)
    arr_ref[A_S2G] = (part + dot(sg_ref[...], ghost_ref[2, :, 0:width])).astype(BF)
    spread(A_S2G)
    last_leg()

    own_copy.wait()

    def build(t, _):
        for j in range(nm):
            c_ref[pl.ds(pl.multiple_of(t * width, width), width), j * width : (j + 1) * width] = cv_ref[j, inv_ref[t, j]]
        return 0

    lax.fori_loop(0, nm, build, 0)

    def gather(k, _):
        j = (m + k) % nm
        for a in range(7):
            buf, row = PLACE[a]
            arrived(got_ref.at[buf, j, pl.ds(row * slab, slab), :], a_recv.at[a, j])
        return 0

    lax.fori_loop(1, nm, gather, 0)

    lanes = 4 * slab

    def turn(j, _):
        rows = pl.ds(pl.multiple_of(j * width, width), width)
        xt = jnp.transpose(got_ref[0, j].astype(F32))
        x_ref[rows, 0:lanes] = (-xt).astype(BF)
        x_ref[rows, lanes : 2 * lanes] = jnp.zeros((width, lanes), BF)
        gt = jnp.transpose(got_ref[1, j].astype(F32))
        lane = lax.broadcasted_iota(jnp.int32, (width, lanes), 1)
        add_ref[rows, :] = gt + jnp.where(lane < slab, pltpu.roll(gt, slab, 1), 0.0)
        return 0

    lax.fori_loop(0, nm, turn, 0)
    m_copy.wait()

    def stage(k, _):
        prod = dot(c_ref[...], x_ref[...])
        rest = add_ref[...] + prod[:, 0:lanes] + prod[:, lanes:]
        high, low = split(rest)
        x_ref[:, 0:lanes] = high
        x_ref[:, lanes:] = low
        prod = dot(m_ref[...], x_ref[...])
        v = prod[:, 0:lanes] + prod[:, lanes:]
        v_ref[...] = v

        def back(j, _):
            rows = pl.ds(pl.multiple_of(j * width, width), width)
            block = v_ref[rows, :]
            back_src[k, j] = jnp.transpose(block)[0:slab, :]
            high, low = split(block)
            x_ref[rows, 0:lanes] = high
            x_ref[rows, lanes:] = low
            add_ref[rows, :] = pltpu.roll(block, lanes - slab, 1)
            return 0

        lax.fori_loop(0, nm, back, 0)

        def out(i, _):
            to = (m + i) % nm
            send(back_src.at[k, to], back_got.at[k, m], b_send.at[k, to], b_recv.at[k, m], s, to)
            return 0

        lax.fori_loop(1, nm, out, 0)
        back_got[k, m] = back_src[k, m]
        return 0

    lax.fori_loop(0, STEPS, stage, 0)

    def line(a, b):
        return jnp.sum(back_src[a] * back_src[b], axis=(0, 1))[None, :]

    pairs = ((0, 0), (0, 1), (1, 1), (0, 2), (1, 2), (2, 2))
    gram = jnp.concatenate([line(a, b) for a, b in pairs] + [jnp.zeros((2, width), F32)], axis=0)
    gram_src[0] = gram
    gram_got[0, m] = gram

    def reduce_mode(k, _):
        to = (m + k) % nm
        send(gram_src.at[0], gram_got.at[0, m], r_send.at[0, to], r_recv.at[0, m], s, to)
        return 0

    lax.fori_loop(1, nm, reduce_mode, 0)

    def got_mode(k, _):
        j = (m + k) % nm
        arrived(gram_got.at[0, j], r_recv.at[0, j])
        return 0

    lax.fori_loop(1, nm, got_mode, 0)
    gram = jnp.sum(gram_got[0, 0:nm], axis=0)
    gram_src[1] = gram
    gram_got[1, s] = gram

    def reduce_space(k, _):
        to = (s + k) % ns
        send(gram_src.at[1], gram_got.at[1, s], r_send.at[1, to], r_recv.at[1, s], to, m)
        return 0

    lax.fori_loop(1, ns, reduce_space, 0)

    def back_in(k, _):
        j = (m + k) % nm
        for a in range(STEPS):
            arrived(back_got.at[a, j], b_recv.at[a, j])
        return 0

    lax.fori_loop(1, nm, back_in, 0)

    def got_space(k, _):
        j = (s + k) % ns
        arrived(gram_got.at[1, j], r_recv.at[1, j])
        return 0

    lax.fori_loop(1, ns, got_space, 0)
    total = jnp.sum(jnp.sum(gram_got[1, 0:ns], axis=0), axis=1, keepdims=True) * (1.0 / (nodes * ns * nm * width))
    g00, g01, g11, g02, g12, g22 = [total[r : r + 1, :] for r in range(6)]

    def damp(mean_square):
        return step_gain / jnp.sqrt(jnp.maximum(mean_square, 0.0) + 1e-06)

    d0 = damp(g00)
    d1 = damp(g00 - 2.0 * d0 * g01 + d0 * d0 * g11)
    p, q = -(d0 + d1), d0 * d1
    d2 = damp(g00 + p * p * g11 + q * q * g22 + 2.0 * (p * g01 + q * g02 + p * q * g12))
    a0 = d0 + d1 + d2
    a1 = -d0 * d1 - d2 * (d0 + d1)
    a2 = q * d2
    for j in range(nm):
        rows = slice(j * slab, (j + 1) * slab)
        o_ref[rows, :] = f_ref[rows, :] + a0 * back_got[0, j] + a1 * back_got[1, j] + a2 * back_got[2, j]

    for r in range(3):
        ghosts_sent(r)

    def drain(k, _):
        to = (m + k) % nm
        for a in range(7):
            sent(arr_ref.at[a, pl.ds(to * slab, slab), :], a_send.at[a, to])
        for a in range(STEPS):
            sent(back_src.at[a, to], b_send.at[a, to])
        sent(gram_src.at[0], r_send.at[0, to])
        sent(table(to, c), c_send.at[nx * nx - 1 + to])
        return 0

    lax.fori_loop(1, nm, drain, 0)

    def drain_space(k, _):
        sent(gram_src.at[1], r_send.at[1, (s + k) % ns])
        return 0

    lax.fori_loop(1, ns, drain_space, 0)

    def drain_table(k, _):
        sent(vals_ref.at[mine], c_send.at[k])
        return 0

    lax.fori_loop(0, nx * nx - 1, drain_table, 0)


def solution(mesh):
    ns, nm = mesh.shape["space"], mesh.shape["mode"]
    nx = int(round(nm ** 0.5))

    def step(guess, forcing, spatial_diag, spatial_ghost, ghost_rows, chaos_vals, chaos_targets, chaos_count, mean_inverse):
        nodes, width = guess.shape
        ghost = ghost_rows.shape[1]
        blocks, slots = chaos_targets.shape
        modes = blocks * width
        slab = nodes // nm
        lanes = 4 * slab
        slot = jnp.arange(slots, dtype=jnp.int32)
        hit = chaos_targets[None, :, :] == jnp.arange(blocks, dtype=jnp.int32)[:, None, None]
        hit = hit & (slot[None, None, :] < chaos_count[None, :, None])
        inverse = slots + jnp.sum(jnp.where(hit, slot[None, None, :] - slots, 0), axis=2)
        vmem = pl.BlockSpec(memory_space=pltpu.VMEM)
        dma = pltpu.SemaphoreType.DMA
        return pl.pallas_call(
            functools.partial(kernel, (ns, nm, nx, slab, ghost, width, slots)),
            out_shape=jax.ShapeDtypeStruct((nodes, width), F32),
            in_specs=[vmem] * 6 + [pl.BlockSpec(memory_space=pltpu.SMEM), pl.BlockSpec(memory_space=pl.ANY)],
            out_specs=vmem,
            scratch_shapes=[
                pltpu.VMEM((modes, modes), BF),
                pltpu.VMEM((modes, modes), BF),
                pltpu.VMEM((nm, slots + 1, width, width), BF),
                pltpu.VMEM((2 * ghost, nodes), BF),
                pltpu.VMEM((7, nodes, width), BF),
                pltpu.VMEM((3, 2 * ghost, 2 * width), BF),
                pltpu.VMEM((3, 2 * ghost, 2 * width), BF),
                pltpu.VMEM((2, nm, lanes, width), BF),
                pltpu.VMEM((modes, 2 * lanes), BF),
                pltpu.VMEM((modes, lanes), F32),
                pltpu.VMEM((modes, lanes), F32),
                pltpu.VMEM((STEPS, nm, slab, width), F32),
                pltpu.VMEM((STEPS, nm, slab, width), F32),
                pltpu.VMEM((2, 8, width), F32),
                pltpu.VMEM((2, max(nm, ns), 8, width), F32),
                dma, dma,
                dma((3, 2)), dma((3, 2)),
                dma((7, nm)), dma((7, nm)),
                dma((nx * nx - 1 + nm,)), dma((nm, 2)),
                dma((STEPS, nm)), dma((STEPS, nm)),
                dma((2, max(nm, ns))), dma((2, max(nm, ns))),
            ],
            compiler_params=pltpu.CompilerParams(
                collective_id=0, has_side_effects=True, vmem_limit_bytes=60 * 2**20
            ),
            name="galerkin",
        )(guess, forcing, spatial_diag, spatial_ghost, ghost_rows, chaos_vals, inverse, mean_inverse)

    space, mode = P("space", "mode"), P("space", None)
    return jax.shard_map(
        step,
        mesh=mesh,
        in_specs=(space, space, mode, mode, mode, P("mode", None, None), P(), P(), P()),
        out_specs=space,
        check_vma=False,
    )
```

```python
import functools

import jax
import jax.numpy as jnp
from jax import lax
from jax.experimental import pallas as pl
from jax.experimental.pallas import tpu as pltpu
from jax.sharding import PartitionSpec as P

STEPS = 3
step_gain = 0.5
BF = jnp.bfloat16
F32 = jnp.float32
A_F, A_SF, A_G, A_GLO, A_SG, A_S2F, A_S2G = range(7)
PLACE = {A_F: (0, 0), A_SF: (0, 1), A_S2F: (0, 2), A_G: (1, 0), A_SG: (1, 1), A_S2G: (1, 2), A_GLO: (1, 3)}


def dot(a, b):
    return jnp.dot(a, b, preferred_element_type=F32)


def split(x):
    high = x.astype(BF)
    return high, (x - high.astype(F32)).astype(BF)


def kernel(
    sizes,
    f_hbm, force_hbm, sd_hbm, sg_hbm, rows_hbm, vals_hbm, target_ref, count_ref, m_hbm,
    o_ref,
    f_ref, force_ref, sd_ref, sg_ref, rows_ref,
    w_ref, cv_ref, slot_ref, inv_ref, oh_ref, arr_ref, gsend_ref, ghost_ref,
    got_ref, x_ref, add_ref, back_src, back_got, gram_src, gram_got,
    l_sem, gh_send, gh_recv, a_send, a_recv, c_send, c_recv, b_send, b_recv, r_send, r_recv,
):
    ns, nm, nx, slab, ghost, width, slots = sizes
    ny = nm // nx
    half = slots // 2
    nodes = f_ref.shape[0]
    s, m = lax.axis_index("space"), lax.axis_index("mode")
    c = s % 2
    y, x = m // nx, m % nx
    mesh = pl.DeviceIdType.MESH

    def send(src, dst, ssem, rsem, to_s, to_m):
        cp = pltpu.make_async_remote_copy(
            src_ref=src, dst_ref=dst, send_sem=ssem, recv_sem=rsem,
            device_id={"space": to_s, "mode": to_m}, device_id_type=mesh,
        )
        cp.start()

    def arrived(dst, rsem):
        pltpu.make_async_remote_copy(
            src_ref=dst, dst_ref=dst, send_sem=rsem, recv_sem=rsem,
            device_id={"space": s, "mode": m}, device_id_type=mesh,
        ).wait_recv()

    def sent(src, ssem):
        pltpu.make_async_remote_copy(
            src_ref=src, dst_ref=src, send_sem=ssem, recv_sem=ssem,
            device_id={"space": s, "mode": m}, device_id_type=mesh,
        ).wait_send()

    barrier = pltpu.get_barrier_semaphore()

    def greet_mode(k, _):
        pl.semaphore_signal(barrier, inc=1, device_id={"space": s, "mode": (m + k) % nm}, device_id_type=mesh)
        return 0

    def greet_space(k, _):
        pl.semaphore_signal(barrier, inc=1, device_id={"space": (s + k) % ns, "mode": m}, device_id_type=mesh)
        return 0

    lax.fori_loop(1, nm, greet_mode, 0)
    lax.fori_loop(1, ns, greet_space, 0)

    loads = [
        pltpu.make_async_copy(src, dst, l_sem.at[n])
        for n, (src, dst) in enumerate((
            (f_hbm, f_ref), (rows_hbm, rows_ref), (vals_hbm, cv_ref.at[m, pl.ds(0, slots)]),
            (sd_hbm, sd_ref), (sg_hbm, sg_ref), (force_hbm, force_ref), (m_hbm, w_ref.at[1]),
        ))
    ]
    for load in loads:
        load.start()
    loads[0].wait()
    loads[1].wait()

    f_bf = f_ref[...].astype(BF)
    arr_ref[A_F] = f_bf
    for side in range(2):
        hits = lax.broadcasted_iota(jnp.int32, (nodes, ghost), 0) == rows_ref[side : side + 1, :]
        picks = jnp.transpose(jnp.where(hits, 1.0, 0.0).astype(F32))
        oh_ref[side * ghost : (side + 1) * ghost, :] = picks.astype(BF)
    picked = dot(oh_ref[...], f_bf).astype(BF)
    gsend_ref[0, :, 0:width] = picked

    def zero_tail(j, _):
        cv_ref[j, slots] = jnp.zeros((width, width), BF)
        got_ref[0, j, pl.ds(3 * slab, slab), :] = jnp.zeros((slab, width), BF)
        add_ref[1, pl.ds(pl.multiple_of(j * width, width), width), :] = jnp.zeros((width, 4 * slab), F32)
        return 0

    lax.fori_loop(0, nm, zero_tail, 0)

    @pl.when(s == 0)
    def _():
        for r in range(3):
            ghost_ref[r, 0:ghost, :] = jnp.zeros((ghost, 2 * width), BF)

    @pl.when(s == ns - 1)
    def _():
        for r in range(3):
            ghost_ref[r, ghost : 2 * ghost, :] = jnp.zeros((ghost, 2 * width), BF)

    pl.semaphore_wait(barrier, nm - 1 + ns - 1)

    wide = [width, 2 * width, width]

    def ghosts_out(r):
        w = wide[r]

        @pl.when(s > 0)
        def _():
            send(gsend_ref.at[r, pl.ds(0, ghost), pl.ds(0, w)], ghost_ref.at[r, pl.ds(ghost, ghost), pl.ds(0, w)],
                 gh_send.at[r, 0], gh_recv.at[r, 1], s - 1, m)

        @pl.when(s < ns - 1)
        def _():
            send(gsend_ref.at[r, pl.ds(ghost, ghost), pl.ds(0, w)], ghost_ref.at[r, pl.ds(0, ghost), pl.ds(0, w)],
                 gh_send.at[r, 1], gh_recv.at[r, 0], s + 1, m)

    def ghosts_in(r):
        w = wide[r]

        @pl.when(s > 0)
        def _():
            arrived(ghost_ref.at[r, pl.ds(0, ghost), pl.ds(0, w)], gh_recv.at[r, 0])

        @pl.when(s < ns - 1)
        def _():
            arrived(ghost_ref.at[r, pl.ds(ghost, ghost), pl.ds(0, w)], gh_recv.at[r, 1])

    def ghosts_sent(r):
        w = wide[r]

        @pl.when(s > 0)
        def _():
            sent(gsend_ref.at[r, pl.ds(0, ghost), pl.ds(0, w)], gh_send.at[r, 0])

        @pl.when(s < ns - 1)
        def _():
            sent(gsend_ref.at[r, pl.ds(ghost, ghost), pl.ds(0, w)], gh_send.at[r, 1])

    def spread(a):
        buf, row = PLACE[a]

        def one(k, _):
            to = (m + k) % nm
            send(arr_ref.at[a, pl.ds(to * slab, slab), :], got_ref.at[buf, m, pl.ds(row * slab, slab), :],
                 a_send.at[a, to], a_recv.at[a, m], s, to)
            return 0

        lax.fori_loop(1, nm, one, 0)
        got_ref[buf, m, pl.ds(row * slab, slab), :] = arr_ref[a, pl.ds(m * slab, slab), :]

    def along(a, b):
        return ((y + a * c + b * (1 - c) + 2 * nx) % ny) * nx + (x + a * (1 - c) + b * c + 2 * nx) % nx

    partner = s + 1 - 2 * c
    leaving = []

    def table(j, h):
        return cv_ref.at[j, pl.ds(h * half, half)]

    def part_of(j, q):
        return cv_ref.at[j, pl.ds(c * half + q * (half // 2), half // 2)]

    def post(ref, j, to_s, to_m):
        sem = c_send.at[len(leaving)]
        leaving.append((ref, sem))
        send(ref, ref, sem, c_recv.at[j, c], to_s, to_m)

    def await_table(a, b):
        j = along(a, b)
        arrived(table(j, c), c_recv.at[j, c])
        post(table(j, c), j, partner, m)
        return j

    def fan_first():
        post(table(m, c), m, s, along(1, 0))
        post(table(m, c), m, s, along(-1, 0))
        post(table(m, c), m, s, along(0, 1))
        post(table(m, c), m, s, along(0, -1))

    def pass_first(a):
        j = await_table(a, 0)
        post(part_of(j, 0 if a < 0 else 1), j, s, along(-a, 0))
        post(table(j, c), j, s, along(0, 1))
        post(table(j, c), j, s, along(0, -1))

    def pass_second(a):
        for b in (-1, 1):
            j = await_table(a, b)
            post(part_of(j, 0 if b < 0 else 1), j, s, along(0, -b))

    def tables_one():
        pass_first(-1)
        pass_first(1)
        pass_second(0)

    def tables_two():
        j = await_table(2, 0)
        post(table(j, c), j, s, along(0, 1))
        post(table(j, c), j, s, along(0, -1))
        pass_second(-1)
        pass_second(1)

    def tables_three():
        pass_second(2)
        for a in (0, -1, 1, 2):
            await_table(a, 2)

    def tables_other():
        def one(k, _):
            j = (m + k) % nm
            arrived(table(j, 1 - c), c_recv.at[j, 1 - c])
            return 0

        lax.fori_loop(1, nm, one, 0)

    ghosts_out(0)
    loads[2].wait()
    fan_first()
    spread(A_F)
    loads[3].wait()
    part = dot(sd_ref[...], f_bf)
    loads[4].wait()
    loads[5].wait()
    ghosts_in(0)
    sf = part + dot(sg_ref[...], ghost_ref[0, :, 0:width])
    g_high, g_low = split(force_ref[...] - sf)
    sf_bf = sf.astype(BF)
    both = jnp.concatenate([g_high, sf_bf], axis=1)
    gsend_ref[1] = dot(oh_ref[...], both).astype(BF)
    ghosts_out(1)
    arr_ref[A_SF] = sf_bf
    arr_ref[A_G] = g_high
    arr_ref[A_GLO] = g_low
    tables_one()
    spread(A_SF)
    spread(A_G)
    spread(A_GLO)
    part = dot(sd_ref[...], both)
    ghosts_in(1)
    two = (part + dot(sg_ref[...], ghost_ref[1])).astype(BF)
    sg_bf = two[:, 0:width]
    gsend_ref[2, :, 0:width] = dot(oh_ref[...], sg_bf).astype(BF)
    ghosts_out(2)
    arr_ref[A_SG] = sg_bf
    arr_ref[A_S2F] = two[:, width : 2 * width]
    spread(A_SG)
    spread(A_S2F)
    tables_two()
    part = dot(sd_ref[...], sg_bf)
    ghosts_in(2)
    arr_ref[A_S2G] = (part + dot(sg_ref[...], ghost_ref[2, :, 0:width])).astype(BF)
    spread(A_S2G)
    tables_three()

    blocks = target_ref.shape[0]
    lane = lax.broadcasted_iota(jnp.int32, (blocks, 128), 1)
    line_no = lax.broadcasted_iota(jnp.int32, (blocks, 128), 0)
    used = jnp.zeros((blocks, 128), jnp.int32)
    for j in range(blocks):
        used = jnp.where(line_no == j, count_ref[j], used)
    found = jnp.full((blocks, 128), slots, jnp.int32)
    for q in range(slots):
        found = jnp.where((target_ref[:, q : q + 1] == lane) & (used > q), q, found)
    slot_ref[...] = found
    table_copy = pltpu.make_async_copy(slot_ref, inv_ref, l_sem.at[7])
    table_copy.start()

    lanes = 4 * slab

    def gather(buf):
        def one(k, _):
            j = (m + k) % nm
            for a in range(7):
                if PLACE[a][0] == buf:
                    arrived(got_ref.at[buf, j, pl.ds(PLACE[a][1] * slab, slab), :], a_recv.at[a, j])
            return 0

        lax.fori_loop(1, nm, one, 0)

    def turn_x(j, _):
        rows = pl.ds(pl.multiple_of(j * width, width), width)
        x_ref[0, rows, 0:lanes] = (-jnp.transpose(got_ref[0, j].astype(F32))).astype(BF)
        x_ref[0, rows, lanes : 2 * lanes] = jnp.zeros((width, lanes), BF)
        return 0

    def turn_g(j, _):
        rows = pl.ds(pl.multiple_of(j * width, width), width)
        gt = jnp.transpose(got_ref[1, j].astype(F32))
        at = lax.broadcasted_iota(jnp.int32, (width, lanes), 1)
        add_ref[0, rows, :] = gt + jnp.where(at < slab, pltpu.roll(gt, slab, 1), 0.0)
        return 0

    gather(0)
    lax.fori_loop(0, nm, turn_x, 0)
    gather(1)
    lax.fori_loop(0, nm, turn_g, 0)
    tables_other()
    table_copy.wait()

    def build(t, _):
        for j in range(nm):
            w_ref[0, pl.ds(pl.multiple_of(t * width, width), width), j * width : (j + 1) * width] = cv_ref[j, inv_ref[j, t]]
        return 0

    lax.fori_loop(0, nm, build, 0)
    loads[6].wait()

    rows_at_once = nm * width // 2

    def apply(p, _):
        odd = p % 2

        def some(q, _):
            base = pl.multiple_of(q * rows_at_once, rows_at_once)
            rows = pl.ds(base, rows_at_once)
            prod = dot(w_ref[odd, rows, :], x_ref[odd])
            value = add_ref[odd, rows, :] + prod[:, 0:lanes] + prod[:, lanes:]
            high, low = split(value)
            x_ref[1 - odd, rows, 0:lanes] = high
            x_ref[1 - odd, rows, lanes:] = low
            add_ref[2 - 2 * odd, rows, :] = pltpu.roll(value, lanes - slab, 1)
            for r in range(nm // 2):
                back_src[p // 2, q * (nm // 2) + r] = jnp.transpose(value[r * width : (r + 1) * width, :])[0:slab, :]
            return 0

        lax.fori_loop(0, 2, some, 0)

        @pl.when((p == 1) | (p == 3))
        def _():
            back_out(p // 2)

        return 0

    def back_out(k):
        def out(i, _):
            to = (m + i) % nm
            send(back_src.at[k, to], back_got.at[k, m], b_send.at[k, to], b_recv.at[k, m], s, to)
            return 0

        lax.fori_loop(1, nm, out, 0)
        back_got[k, m] = back_src[k, m]

    lax.fori_loop(0, 2 * STEPS, apply, 0)

    def line(a, b):
        return jnp.sum(back_src[a] * back_src[b], axis=(0, 1))[None, :]

    pairs = ((0, 0), (0, 1), (1, 1), (0, 2), (1, 2), (2, 2))
    gram = jnp.concatenate([line(a, b) for a, b in pairs] + [jnp.zeros((2, width), F32)], axis=0)
    gram_src[0] = gram
    gram_got[0, m] = gram

    def reduce_mode(k, _):
        to = (m + k) % nm
        send(gram_src.at[0], gram_got.at[0, m], r_send.at[0, to], r_recv.at[0, m], s, to)
        return 0

    lax.fori_loop(1, nm, reduce_mode, 0)
    back_out(STEPS - 1)

    def got_mode(k, _):
        j = (m + k) % nm
        arrived(gram_got.at[0, j], r_recv.at[0, j])
        return 0

    lax.fori_loop(1, nm, got_mode, 0)
    gram = jnp.sum(gram_got[0, 0:nm], axis=0)
    gram_src[1] = gram
    gram_got[1, s] = gram

    def reduce_space(k, _):
        to = (s + k) % ns
        send(gram_src.at[1], gram_got.at[1, s], r_send.at[1, to], r_recv.at[1, s], to, m)
        return 0

    lax.fori_loop(1, ns, reduce_space, 0)

    def back_in(k, _):
        j = (m + k) % nm
        for a in range(STEPS):
            arrived(back_got.at[a, j], b_recv.at[a, j])
        return 0

    lax.fori_loop(1, nm, back_in, 0)

    def got_space(k, _):
        j = (s + k) % ns
        arrived(gram_got.at[1, j], r_recv.at[1, j])
        return 0

    lax.fori_loop(1, ns, got_space, 0)
    total = jnp.sum(jnp.sum(gram_got[1, 0:ns], axis=0), axis=1, keepdims=True) * (1.0 / (nodes * ns * nm * width))
    g00, g01, g11, g02, g12, g22 = [total[r : r + 1, :] for r in range(6)]

    def damp(mean_square):
        return step_gain / jnp.sqrt(jnp.maximum(mean_square, 0.0) + 1e-06)

    d0 = damp(g00)
    d1 = damp(g00 - 2.0 * d0 * g01 + d0 * d0 * g11)
    p, q = -(d0 + d1), d0 * d1
    d2 = damp(g00 + p * p * g11 + q * q * g22 + 2.0 * (p * g01 + q * g02 + p * q * g12))
    a0 = d0 + d1 + d2
    a1 = -d0 * d1 - d2 * (d0 + d1)
    a2 = q * d2
    o_ref[...] = a0 * back_got[0] + a1 * back_got[1] + a2 * back_got[2]

    for r in range(3):
        ghosts_sent(r)

    def drain(k, _):
        to = (m + k) % nm
        for a in range(7):
            sent(arr_ref.at[a, pl.ds(to * slab, slab), :], a_send.at[a, to])
        for a in range(STEPS):
            sent(back_src.at[a, to], b_send.at[a, to])
        sent(gram_src.at[0], r_send.at[0, to])
        return 0

    lax.fori_loop(1, nm, drain, 0)

    def drain_space(k, _):
        sent(gram_src.at[1], r_send.at[1, (s + k) % ns])
        return 0

    lax.fori_loop(1, ns, drain_space, 0)

    for ref, sem in leaving:
        sent(ref, sem)


def solution(mesh):
    ns, nm = mesh.shape["space"], mesh.shape["mode"]
    nx = int(round(nm ** 0.5))

    def step(guess, forcing, spatial_diag, spatial_ghost, ghost_rows, chaos_vals, chaos_targets, chaos_count, mean_inverse):
        nodes, width = guess.shape
        ghost = ghost_rows.shape[1]
        blocks, slots = chaos_targets.shape
        modes = blocks * width
        slab = nodes // nm
        lanes = 4 * slab
        vmem = pl.BlockSpec(memory_space=pltpu.VMEM)
        dma = pltpu.SemaphoreType.DMA
        smem, anywhere = pl.BlockSpec(memory_space=pltpu.SMEM), pl.BlockSpec(memory_space=pl.ANY)
        gathered = pl.pallas_call(
            functools.partial(kernel, (ns, nm, nx, slab, ghost, width, slots)),
            out_shape=jax.ShapeDtypeStruct((nm, slab, width), F32),
            in_specs=[anywhere] * 6 + [vmem, smem, anywhere],
            out_specs=vmem,
            scratch_shapes=[
                pltpu.VMEM((nodes, width), F32),
                pltpu.VMEM((nodes, width), F32),
                pltpu.VMEM((nodes, nodes), BF),
                pltpu.VMEM((nodes, 2 * ghost), BF),
                pltpu.VMEM((2, ghost), jnp.int32),
                pltpu.VMEM((2, modes, modes), BF),
                pltpu.VMEM((nm, slots + 1, width, width), BF),
                pltpu.VMEM((blocks, 128), jnp.int32),
                pltpu.SMEM((blocks, 128), jnp.int32),
                pltpu.VMEM((2 * ghost, nodes), BF),
                pltpu.VMEM((7, nodes, width), BF),
                pltpu.VMEM((3, 2 * ghost, 2 * width), BF),
                pltpu.VMEM((3, 2 * ghost, 2 * width), BF),
                pltpu.VMEM((2, nm, lanes, width), BF),
                pltpu.VMEM((2, modes, 2 * lanes), BF),
                pltpu.VMEM((3, modes, lanes), F32),
                pltpu.VMEM((STEPS, nm, slab, width), F32),
                pltpu.VMEM((STEPS, nm, slab, width), F32),
                pltpu.VMEM((2, 8, width), F32),
                pltpu.VMEM((2, max(nm, ns), 8, width), F32),
                dma((8,)),
                dma((3, 2)), dma((3, 2)),
                dma((7, nm)), dma((7, nm)),
                dma((40,)), dma((nm, 2)),
                dma((STEPS, nm)), dma((STEPS, nm)),
                dma((2, max(nm, ns))), dma((2, max(nm, ns))),
            ],
            compiler_params=pltpu.CompilerParams(
                collective_id=0, has_side_effects=True, vmem_limit_bytes=60 * 2**20
            ),
            name="galerkin",
        )(guess, forcing, spatial_diag, spatial_ghost, ghost_rows, chaos_vals, chaos_targets, chaos_count, mean_inverse)
        return guess + gathered.reshape(nodes, width)

    space, mode = P("space", "mode"), P("space", None)
    return jax.shard_map(
        step,
        mesh=mesh,
        in_specs=(space, space, mode, mode, mode, P("mode", None, None), P(), P(), P()),
        out_specs=space,
        check_vma=False,
    )
```

```python
import functools

import jax
import jax.numpy as jnp
from jax import lax
from jax.experimental import pallas as pl
from jax.experimental.pallas import tpu as pltpu
from jax.sharding import PartitionSpec as P

STEPS = 3
step_gain = 0.5
BF = jnp.bfloat16
F32 = jnp.float32
A_F, A_SF, A_G, A_GLO, A_SG, A_S2F, A_S2G = range(7)
PLACE = {A_F: (0, 0), A_SF: (0, 1), A_S2F: (0, 2), A_G: (1, 0), A_SG: (1, 1), A_S2G: (1, 2), A_GLO: (1, 3)}


def dot(a, b):
    return jnp.dot(a, b, preferred_element_type=F32)


def split(x):
    high = x.astype(BF)
    return high, (x - high.astype(F32)).astype(BF)


def kernel(
    sizes,
    f_hbm, force_hbm, sd_hbm, sg_hbm, rows_hbm, vals_hbm, target_ref, count_ref, m_hbm,
    o_ref,
    f_ref, force_ref, sd_ref, sg_ref, rows_ref,
    w_ref, cv_ref, slot_ref, inv_ref, oh_ref, arr_ref, gsend_ref, ghost_ref,
    got_ref, x_ref, add_ref, back_src, back_got, last_src, last_got, gram_src, gram_got,
    l_sem, gh_send, gh_recv, a_send, a_recv, c_send, z_send, c_recv, b_send, b_recv, r_send, r_recv,
):
    ns, nm, nx, slab, ghost, width, slots = sizes
    ny = nm // nx
    nodes = f_ref.shape[0]
    s, m = lax.axis_index("space"), lax.axis_index("mode")
    c = s % 2
    y, x = m // nx, m % nx
    mesh = pl.DeviceIdType.MESH

    def send(src, dst, ssem, rsem, to_s, to_m):
        cp = pltpu.make_async_remote_copy(
            src_ref=src, dst_ref=dst, send_sem=ssem, recv_sem=rsem,
            device_id={"space": to_s, "mode": to_m}, device_id_type=mesh,
        )
        cp.start()

    def arrived(dst, rsem):
        pltpu.make_async_remote_copy(
            src_ref=dst, dst_ref=dst, send_sem=rsem, recv_sem=rsem,
            device_id={"space": s, "mode": m}, device_id_type=mesh,
        ).wait_recv()

    def sent(src, ssem):
        pltpu.make_async_remote_copy(
            src_ref=src, dst_ref=src, send_sem=ssem, recv_sem=ssem,
            device_id={"space": s, "mode": m}, device_id_type=mesh,
        ).wait_send()

    barrier = pltpu.get_barrier_semaphore()

    def greet_mode(k, _):
        pl.semaphore_signal(barrier, inc=1, device_id={"space": s, "mode": (m + k) % nm}, device_id_type=mesh)
        return 0

    def greet_space(k, _):
        pl.semaphore_signal(barrier, inc=1, device_id={"space": (s + k) % ns, "mode": m}, device_id_type=mesh)
        return 0

    lax.fori_loop(1, nm, greet_mode, 0)
    lax.fori_loop(1, ns, greet_space, 0)

    loads = [
        pltpu.make_async_copy(src, dst, l_sem.at[n])
        for n, (src, dst) in enumerate((
            (f_hbm, f_ref), (rows_hbm, rows_ref), (vals_hbm, cv_ref.at[m, pl.ds(0, slots)]),
            (sd_hbm, sd_ref), (sg_hbm, sg_ref), (force_hbm, force_ref), (m_hbm, w_ref.at[1]),
        ))
    ]
    for load in loads:
        load.start()
    loads[0].wait()
    loads[1].wait()

    f_bf = f_ref[...].astype(BF)
    arr_ref[A_F] = f_bf
    for side in range(2):
        hits = lax.broadcasted_iota(jnp.int32, (nodes, ghost), 0) == rows_ref[side : side + 1, :]
        picks = jnp.transpose(jnp.where(hits, 1.0, 0.0).astype(F32))
        oh_ref[side * ghost : (side + 1) * ghost, :] = picks.astype(BF)
    picked = dot(oh_ref[...], f_bf).astype(BF)
    gsend_ref[0, :, 0:width] = picked

    def zero_tail(j, _):
        cv_ref[j, slots] = jnp.zeros((width, width), BF)
        got_ref[0, j, pl.ds(3 * slab, slab), :] = jnp.zeros((slab, width), BF)
        add_ref[1, pl.ds(pl.multiple_of(j * width, width), width), :] = jnp.zeros((width, 4 * slab), F32)
        return 0

    lax.fori_loop(0, nm, zero_tail, 0)

    @pl.when(s == 0)
    def _():
        for r in range(3):
            ghost_ref[r, 0:ghost, :] = jnp.zeros((ghost, 2 * width), BF)

    @pl.when(s == ns - 1)
    def _():
        for r in range(3):
            ghost_ref[r, ghost : 2 * ghost, :] = jnp.zeros((ghost, 2 * width), BF)

    loads[3].wait()
    part = dot(sd_ref[...], f_bf)
    pl.semaphore_wait(barrier, nm - 1 + ns - 1)

    wide = [width, 2 * width, width]

    def ghosts_out(r):
        w = wide[r]

        @pl.when(s > 0)
        def _():
            send(gsend_ref.at[r, pl.ds(0, ghost), pl.ds(0, w)], ghost_ref.at[r, pl.ds(ghost, ghost), pl.ds(0, w)],
                 gh_send.at[r, 0], gh_recv.at[r, 1], s - 1, m)

        @pl.when(s < ns - 1)
        def _():
            send(gsend_ref.at[r, pl.ds(ghost, ghost), pl.ds(0, w)], ghost_ref.at[r, pl.ds(0, ghost), pl.ds(0, w)],
                 gh_send.at[r, 1], gh_recv.at[r, 0], s + 1, m)

    def ghosts_in(r):
        w = wide[r]

        @pl.when(s > 0)
        def _():
            arrived(ghost_ref.at[r, pl.ds(0, ghost), pl.ds(0, w)], gh_recv.at[r, 0])

        @pl.when(s < ns - 1)
        def _():
            arrived(ghost_ref.at[r, pl.ds(ghost, ghost), pl.ds(0, w)], gh_recv.at[r, 1])

    def ghosts_sent(r):
        w = wide[r]

        @pl.when(s > 0)
        def _():
            sent(gsend_ref.at[r, pl.ds(0, ghost), pl.ds(0, w)], gh_send.at[r, 0])

        @pl.when(s < ns - 1)
        def _():
            sent(gsend_ref.at[r, pl.ds(ghost, ghost), pl.ds(0, w)], gh_send.at[r, 1])

    def spread(a):
        buf, row = PLACE[a]

        def one(k, _):
            to = (m + k) % nm
            send(arr_ref.at[a, pl.ds(to * slab, slab), :], got_ref.at[buf, m, pl.ds(row * slab, slab), :],
                 a_send.at[a, to], a_recv.at[a, m], s, to)
            return 0

        lax.fori_loop(1, nm, one, 0)
        got_ref[buf, m, pl.ds(row * slab, slab), :] = arr_ref[a, pl.ds(m * slab, slab), :]

    pair = slots // 4
    level = (s // 2) % 2
    base, far = level * 2 * pair + c * pair, (1 - level) * 2 * pair + c * pair
    partner, above, below = s + 1 - 2 * c, (s + 2) % ns, (s + ns - 2) % ns
    leaving = []

    def along(a, b):
        return ((y + a * c + b * (1 - c) + 2 * nx) % ny) * nx + (x + a * (1 - c) + b * c + 2 * nx) % nx

    def table(j, first, count=pair):
        return cv_ref.at[j, pl.ds(first, count)]

    def post(ref, j, kind, to_s, to_m):
        sem = c_send.at[len(leaving)]
        leaving.append((ref, sem))
        send(ref, ref, sem, c_recv.at[j, kind], to_s, to_m)

    def await_table(a, b):
        j = along(a, b)
        arrived(table(j, base), c_recv.at[j, 0])
        return j

    def share(j):
        post(table(j, base, pair // 2), j, 1, above, m)
        post(table(j, base + pair // 2, pair // 2), j, 1, below, m)
        post(table(j, base), j, 2, partner, m)

    def both_ways(j):
        post(table(j, base), j, 0, s, along(0, 1))
        post(table(j, base), j, 0, s, along(0, -1))

    def fan_first():
        post(table(m, base), m, 0, s, along(1, 0))
        post(table(m, base), m, 0, s, along(-1, 0))
        both_ways(m)

    def pass_first(a):
        j = await_table(a, 0)
        post(table(j, base + (0 if a < 0 else pair // 2), pair // 2), j, 0, s, along(-a, 0))
        both_ways(j)
        share(j)

    def pass_second(a):
        for b in (-1, 1):
            j = await_table(a, b)
            post(table(j, base + (0 if b < 0 else pair // 2), pair // 2), j, 0, s, along(0, -b))
            share(j)

    def tables_one():
        pass_first(-1)
        pass_first(1)
        pass_second(0)

    def tables_two():
        j = await_table(2, 0)
        both_ways(j)
        share(j)
        pass_second(-1)
        pass_second(1)

    def tables_three():
        pass_second(2)
        for a in (0, -1, 1, 2):
            share(await_table(a, 2))

    def tables_other():
        def level_in(k, _):
            j = (m + k) % nm
            arrived(table(j, far), c_recv.at[j, 1])
            send(table(j, far), table(j, far), z_send.at[j], c_recv.at[j, 3], partner, m)
            return 0

        lax.fori_loop(1, nm, level_in, 0)

        def core_in(k, _):
            j = (m + k) % nm
            arrived(table(j, base + pair - 2 * c * pair), c_recv.at[j, 2])
            arrived(table(j, far + pair - 2 * c * pair), c_recv.at[j, 3])
            return 0

        lax.fori_loop(1, nm, core_in, 0)

    ghosts_out(0)
    loads[2].wait()
    fan_first()
    spread(A_F)
    loads[4].wait()
    loads[5].wait()
    ghosts_in(0)
    sf = part + dot(sg_ref[...], ghost_ref[0, :, 0:width])
    g_high, g_low = split(force_ref[...] - sf)
    sf_bf = sf.astype(BF)
    both = jnp.concatenate([g_high, sf_bf], axis=1)
    gsend_ref[1] = dot(oh_ref[...], both).astype(BF)
    ghosts_out(1)
    arr_ref[A_SF] = sf_bf
    arr_ref[A_G] = g_high
    arr_ref[A_GLO] = g_low
    tables_one()
    spread(A_SF)
    spread(A_G)
    spread(A_GLO)
    part = dot(sd_ref[...], both)
    ghosts_in(1)
    two = (part + dot(sg_ref[...], ghost_ref[1])).astype(BF)
    sg_bf = two[:, 0:width]
    gsend_ref[2, :, 0:width] = dot(oh_ref[...], sg_bf).astype(BF)
    ghosts_out(2)
    arr_ref[A_SG] = sg_bf
    arr_ref[A_S2F] = two[:, width : 2 * width]
    spread(A_SG)
    spread(A_S2F)
    tables_two()
    part = dot(sd_ref[...], sg_bf)
    ghosts_in(2)
    arr_ref[A_S2G] = (part + dot(sg_ref[...], ghost_ref[2, :, 0:width])).astype(BF)
    spread(A_S2G)
    tables_three()

    blocks = target_ref.shape[1]
    lane = lax.broadcasted_iota(jnp.int32, (blocks, blocks), 1)
    goal = lax.broadcasted_iota(jnp.int32, (blocks, blocks), 0)
    used = jnp.zeros((blocks, blocks), jnp.int32)
    for j in range(blocks):
        used = jnp.where(lane == j, count_ref[j], used)
    found = jnp.full((blocks, blocks), slots, jnp.int32)
    for q in range(slots):
        found = jnp.where((target_ref[q : q + 1, :] == goal) & (used > q), q, found)
    slot_ref[...] = jnp.zeros((blocks, 128), jnp.int32)
    slot_ref[:, 0:blocks] = found
    table_copy = pltpu.make_async_copy(slot_ref, inv_ref, l_sem.at[7])
    table_copy.start()

    lanes = 4 * slab

    def gather(buf):
        def one(k, _):
            j = (m + k) % nm
            for a in range(7):
                if PLACE[a][0] == buf:
                    arrived(got_ref.at[buf, j, pl.ds(PLACE[a][1] * slab, slab), :], a_recv.at[a, j])
            return 0

        lax.fori_loop(1, nm, one, 0)

    def turn_x(j, _):
        rows = pl.ds(pl.multiple_of(j * width, width), width)
        x_ref[0, rows, 0:lanes] = (-jnp.transpose(got_ref[0, j].astype(F32))).astype(BF)
        x_ref[0, rows, lanes : 2 * lanes] = jnp.zeros((width, lanes), BF)
        return 0

    def turn_g(j, _):
        rows = pl.ds(pl.multiple_of(j * width, width), width)
        gt = jnp.transpose(got_ref[1, j].astype(F32))
        at = lax.broadcasted_iota(jnp.int32, (width, lanes), 1)
        add_ref[0, rows, :] = gt + jnp.where(at < slab, pltpu.roll(gt, slab, 1), 0.0)
        return 0

    gather(0)
    lax.fori_loop(0, nm, turn_x, 0)
    gather(1)
    lax.fori_loop(0, nm, turn_g, 0)
    tables_other()
    table_copy.wait()

    def build(t, _):
        for j in range(nm):
            w_ref[0, pl.ds(pl.multiple_of(t * width, width), width), j * width : (j + 1) * width] = cv_ref[j, inv_ref[t, j]]
        return 0

    lax.fori_loop(0, nm, build, 0)
    loads[6].wait()

    rows_at_once = nm * width // 2

    def apply(p, _):
        odd = p % 2

        def some(q, _):
            base = pl.multiple_of(q * rows_at_once, rows_at_once)
            rows = pl.ds(base, rows_at_once)
            prod = dot(w_ref[odd, rows, :], x_ref[odd])
            value = add_ref[odd, rows, :] + prod[:, 0:lanes] + prod[:, lanes:]
            high, low = split(value)
            x_ref[1 - odd, rows, 0:lanes] = high
            x_ref[1 - odd, rows, lanes:] = low
            add_ref[2 - 2 * odd, rows, :] = pltpu.roll(value, lanes - slab, 1)
            return 0

        lax.fori_loop(0, 2, some, 0)

        @pl.when(odd == 1)
        def _():
            def turn_back(j, _):
                block = add_ref[0, pl.ds(pl.multiple_of(j * width, width), width), :]
                back_src[p // 2, j] = jnp.transpose(block)[lanes - slab :, :]
                return 0

            lax.fori_loop(0, nm, turn_back, 0, unroll=2)

        @pl.when((p == 1) | (p == 3))
        def _():
            back_out(p // 2)

        return 0

    def back_dst(a, many, one):
        return one if isinstance(a, int) and a == STEPS - 1 else many.at[a]

    def back_out(k):
        src, dst = back_dst(k, back_src, last_src), back_dst(k, back_got, last_got)

        def out(i, _):
            to = (m + i) % nm
            send(src.at[to], dst.at[m], b_send.at[k, to], b_recv.at[k, m], s, to)
            return 0

        lax.fori_loop(1, nm, out, 0)
        dst[m] = src[m]

    lax.fori_loop(0, 2 * STEPS, apply, 0)

    def line(a, b):
        return jnp.sum(back_src[a] * back_src[b], axis=(0, 1))[None, :]

    pairs = ((0, 0), (0, 1), (1, 1), (0, 2), (1, 2), (2, 2))
    gram = jnp.concatenate([line(a, b) for a, b in pairs] + [jnp.zeros((2, width), F32)], axis=0)
    gram_src[0] = gram
    gram_got[0, m] = gram

    def reduce_mode(k, _):
        to = (m + k) % nm
        send(gram_src.at[0], gram_got.at[0, m], r_send.at[0, to], r_recv.at[0, m], s, to)
        return 0

    lax.fori_loop(1, nm, reduce_mode, 0)
    last_src[...] = back_src[STEPS - 1].astype(BF)
    back_out(STEPS - 1)

    def got_mode(k, _):
        j = (m + k) % nm
        arrived(gram_got.at[0, j], r_recv.at[0, j])
        return 0

    lax.fori_loop(1, nm, got_mode, 0)
    gram = jnp.sum(gram_got[0, 0:nm], axis=0)
    gram_src[1] = gram
    gram_got[1, s] = gram

    def reduce_space(k, _):
        to = (s + k) % ns
        send(gram_src.at[1], gram_got.at[1, s], r_send.at[1, to], r_recv.at[1, s], to, m)
        return 0

    lax.fori_loop(1, ns, reduce_space, 0)

    def back_in(k, _):
        j = (m + k) % nm
        for a in range(STEPS):
            arrived(back_dst(a, back_got, last_got).at[j], b_recv.at[a, j])
        return 0

    lax.fori_loop(1, nm, back_in, 0)

    def got_space(k, _):
        j = (s + k) % ns
        arrived(gram_got.at[1, j], r_recv.at[1, j])
        return 0

    lax.fori_loop(1, ns, got_space, 0)
    total = jnp.sum(jnp.sum(gram_got[1, 0:ns], axis=0), axis=1, keepdims=True) * (1.0 / (nodes * ns * nm * width))
    g00, g01, g11, g02, g12, g22 = [total[r : r + 1, :] for r in range(6)]

    def damp(mean_square):
        return step_gain / jnp.sqrt(jnp.maximum(mean_square, 0.0) + 1e-06)

    d0 = damp(g00)
    d1 = damp(g00 - 2.0 * d0 * g01 + d0 * d0 * g11)
    p, q = -(d0 + d1), d0 * d1
    d2 = damp(g00 + p * p * g11 + q * q * g22 + 2.0 * (p * g01 + q * g02 + p * q * g12))
    a0 = d0 + d1 + d2
    a1 = -d0 * d1 - d2 * (d0 + d1)
    a2 = q * d2
    o_ref[...] = a0 * back_got[0] + a1 * back_got[1] + a2 * last_got[...].astype(F32)

    for r in range(3):
        ghosts_sent(r)

    def drain(k, _):
        to = (m + k) % nm
        for a in range(7):
            sent(arr_ref.at[a, pl.ds(to * slab, slab), :], a_send.at[a, to])
        for a in range(STEPS):
            sent(back_dst(a, back_src, last_src).at[to], b_send.at[a, to])
        sent(gram_src.at[0], r_send.at[0, to])
        sent(table(to, far), z_send.at[to])
        return 0

    lax.fori_loop(1, nm, drain, 0)

    def drain_space(k, _):
        sent(gram_src.at[1], r_send.at[1, (s + k) % ns])
        return 0

    lax.fori_loop(1, ns, drain_space, 0)

    for ref, sem in leaving:
        sent(ref, sem)


def solution(mesh):
    ns, nm = mesh.shape["space"], mesh.shape["mode"]
    nx = int(round(nm ** 0.5))

    def step(guess, forcing, spatial_diag, spatial_ghost, ghost_rows, chaos_vals, chaos_targets, chaos_count, mean_inverse):
        nodes, width = guess.shape
        ghost = ghost_rows.shape[1]
        blocks, slots = chaos_targets.shape
        modes = blocks * width
        slab = nodes // nm
        lanes = 4 * slab
        vmem = pl.BlockSpec(memory_space=pltpu.VMEM)
        dma = pltpu.SemaphoreType.DMA
        smem, anywhere = pl.BlockSpec(memory_space=pltpu.SMEM), pl.BlockSpec(memory_space=pl.ANY)
        gathered = pl.pallas_call(
            functools.partial(kernel, (ns, nm, nx, slab, ghost, width, slots)),
            out_shape=jax.ShapeDtypeStruct((nm, slab, width), F32),
            in_specs=[anywhere] * 6 + [vmem, smem, anywhere],
            out_specs=vmem,
            scratch_shapes=[
                pltpu.VMEM((nodes, width), F32),
                pltpu.VMEM((nodes, width), F32),
                pltpu.VMEM((nodes, nodes), BF),
                pltpu.VMEM((nodes, 2 * ghost), BF),
                pltpu.VMEM((2, ghost), jnp.int32),
                pltpu.VMEM((2, modes, modes), BF),
                pltpu.VMEM((nm, slots + 1, width, width), BF),
                pltpu.VMEM((blocks, 128), jnp.int32),
                pltpu.SMEM((blocks, 128), jnp.int32),
                pltpu.VMEM((2 * ghost, nodes), BF),
                pltpu.VMEM((7, nodes, width), BF),
                pltpu.VMEM((3, 2 * ghost, 2 * width), BF),
                pltpu.VMEM((3, 2 * ghost, 2 * width), BF),
                pltpu.VMEM((2, nm, lanes, width), BF),
                pltpu.VMEM((2, modes, 2 * lanes), BF),
                pltpu.VMEM((3, modes, lanes), F32),
                pltpu.VMEM((STEPS, nm, slab, width), F32),
                pltpu.VMEM((STEPS - 1, nm, slab, width), F32),
                pltpu.VMEM((nm, slab, width), BF),
                pltpu.VMEM((nm, slab, width), BF),
                pltpu.VMEM((2, 8, width), F32),
                pltpu.VMEM((2, max(nm, ns), 8, width), F32),
                dma((8,)),
                dma((3, 2)), dma((3, 2)),
                dma((7, nm)), dma((7, nm)),
                dma((72,)), dma((nm,)), dma((nm, 4)),
                dma((STEPS, nm)), dma((STEPS, nm)),
                dma((2, max(nm, ns))), dma((2, max(nm, ns))),
            ],
            compiler_params=pltpu.CompilerParams(
                collective_id=0, has_side_effects=True, vmem_limit_bytes=60 * 2**20
            ),
            name="galerkin",
        )(guess, forcing, spatial_diag, spatial_ghost, ghost_rows, chaos_vals, chaos_targets.T, chaos_count, mean_inverse)
        return guess + gathered.reshape(nodes, width)

    space, mode = P("space", "mode"), P("space", None)
    return jax.shard_map(
        step,
        mesh=mesh,
        in_specs=(space, space, mode, mode, mode, P("mode", None, None), P(), P(), P()),
        out_specs=space,
        check_vma=False,
    )
```

```python
import functools

import jax
import jax.numpy as jnp
from jax import lax
from jax.experimental import pallas as pl
from jax.experimental.pallas import tpu as pltpu
from jax.sharding import PartitionSpec as P

STEPS = 3
step_gain = 0.5
BF = jnp.bfloat16
F32 = jnp.float32
A_F, A_SF, A_G, A_GLO, A_SG, A_S2F, A_S2G = range(7)
PLACE = {A_F: (0, 0), A_SF: (0, 1), A_S2F: (0, 2), A_G: (1, 0), A_SG: (1, 1), A_S2G: (1, 2), A_GLO: (1, 3)}


def dot(a, b):
    return jnp.dot(a, b, preferred_element_type=F32)


def split(x):
    high = x.astype(BF)
    return high, (x - high.astype(F32)).astype(BF)


def kernel(
    sizes,
    f_hbm, force_hbm, sd_hbm, sg_hbm, rows_hbm, vals_hbm, target_ref, count_ref, m_hbm,
    o_ref,
    f_ref, force_ref, sd_ref, sg_ref, rows_ref,
    w_ref, cv_ref, slot_ref, inv_ref, oh_ref, arr_ref, gsend_ref, ghost_ref,
    got_ref, x_ref, add_ref, back_src, back_got, last_src, last_got, gram_src, gram_got,
    l_sem, gh_send, gh_recv, a_send, a_recv, c_send, c_recv, p_recv, b_send, b_recv, r_send, r_recv,
):
    ns, nm, nx, slab, ghost, width, slots = sizes
    ny = nm // nx
    nodes = f_ref.shape[0]
    s, m = lax.axis_index("space"), lax.axis_index("mode")
    c = s % 2
    y, x = m // nx, m % nx
    mesh = pl.DeviceIdType.MESH

    def send(src, dst, ssem, rsem, to_s, to_m):
        cp = pltpu.make_async_remote_copy(
            src_ref=src, dst_ref=dst, send_sem=ssem, recv_sem=rsem,
            device_id={"space": to_s, "mode": to_m}, device_id_type=mesh,
        )
        cp.start()

    def arrived(dst, rsem):
        pltpu.make_async_remote_copy(
            src_ref=dst, dst_ref=dst, send_sem=rsem, recv_sem=rsem,
            device_id={"space": s, "mode": m}, device_id_type=mesh,
        ).wait_recv()

    def sent(src, ssem):
        pltpu.make_async_remote_copy(
            src_ref=src, dst_ref=src, send_sem=ssem, recv_sem=ssem,
            device_id={"space": s, "mode": m}, device_id_type=mesh,
        ).wait_send()

    barrier = pltpu.get_barrier_semaphore()

    def greet_mode(k, _):
        pl.semaphore_signal(barrier, inc=1, device_id={"space": s, "mode": (m + k) % nm}, device_id_type=mesh)
        return 0

    def greet_space(k, _):
        pl.semaphore_signal(barrier, inc=1, device_id={"space": (s + k) % ns, "mode": m}, device_id_type=mesh)
        return 0

    lax.fori_loop(1, nm, greet_mode, 0)
    lax.fori_loop(1, ns, greet_space, 0)

    loads = [
        pltpu.make_async_copy(src, dst, l_sem.at[n])
        for n, (src, dst) in enumerate((
            (f_hbm, f_ref), (rows_hbm, rows_ref), (vals_hbm, cv_ref.at[m, pl.ds(0, slots)]),
            (sd_hbm, sd_ref), (sg_hbm, sg_ref), (force_hbm, force_ref), (m_hbm, w_ref.at[1]),
        ))
    ]
    for load in loads:
        load.start()
    loads[0].wait()
    loads[1].wait()

    f_bf = f_ref[...].astype(BF)
    arr_ref[A_F] = f_bf
    for side in range(2):
        hits = lax.broadcasted_iota(jnp.int32, (nodes, ghost), 0) == rows_ref[side : side + 1, :]
        picks = jnp.transpose(jnp.where(hits, 1.0, 0.0).astype(F32))
        oh_ref[side * ghost : (side + 1) * ghost, :] = picks.astype(BF)
    picked = dot(oh_ref[...], f_bf).astype(BF)
    gsend_ref[0, :, 0:width] = picked

    def zero_tail(j, _):
        cv_ref[j, slots] = jnp.zeros((width, width), BF)
        got_ref[0, j, pl.ds(3 * slab, slab), :] = jnp.zeros((slab, width), BF)
        add_ref[1, pl.ds(pl.multiple_of(j * width, width), width), :] = jnp.zeros((width, 4 * slab), F32)
        return 0

    lax.fori_loop(0, nm, zero_tail, 0)

    @pl.when(s == 0)
    def _():
        for r in range(3):
            ghost_ref[r, 0:ghost, :] = jnp.zeros((ghost, 2 * width), BF)

    @pl.when(s == ns - 1)
    def _():
        for r in range(3):
            ghost_ref[r, ghost : 2 * ghost, :] = jnp.zeros((ghost, 2 * width), BF)

    loads[3].wait()
    part = dot(sd_ref[...], f_bf)
    pl.semaphore_wait(barrier, nm - 1 + ns - 1)

    wide = [width, 2 * width, width]

    def ghosts_out(r):
        w = wide[r]

        @pl.when(s > 0)
        def _():
            send(gsend_ref.at[r, pl.ds(0, ghost), pl.ds(0, w)], ghost_ref.at[r, pl.ds(ghost, ghost), pl.ds(0, w)],
                 gh_send.at[r, 0], gh_recv.at[r, 1], s - 1, m)

        @pl.when(s < ns - 1)
        def _():
            send(gsend_ref.at[r, pl.ds(ghost, ghost), pl.ds(0, w)], ghost_ref.at[r, pl.ds(0, ghost), pl.ds(0, w)],
                 gh_send.at[r, 1], gh_recv.at[r, 0], s + 1, m)

    def ghosts_in(r):
        w = wide[r]

        @pl.when(s > 0)
        def _():
            arrived(ghost_ref.at[r, pl.ds(0, ghost), pl.ds(0, w)], gh_recv.at[r, 0])

        @pl.when(s < ns - 1)
        def _():
            arrived(ghost_ref.at[r, pl.ds(ghost, ghost), pl.ds(0, w)], gh_recv.at[r, 1])

    def ghosts_sent(r):
        w = wide[r]

        @pl.when(s > 0)
        def _():
            sent(gsend_ref.at[r, pl.ds(0, ghost), pl.ds(0, w)], gh_send.at[r, 0])

        @pl.when(s < ns - 1)
        def _():
            sent(gsend_ref.at[r, pl.ds(ghost, ghost), pl.ds(0, w)], gh_send.at[r, 1])

    def spread(a):
        buf, row = PLACE[a]

        def one(k, _):
            to = (m + k) % nm
            send(arr_ref.at[a, pl.ds(to * slab, slab), :], got_ref.at[buf, m, pl.ds(row * slab, slab), :],
                 a_send, a_recv.at[buf], s, to)
            return 0

        lax.fori_loop(1, nm, one, 0)
        got_ref[buf, m, pl.ds(row * slab, slab), :] = arr_ref[a, pl.ds(m * slab, slab), :]

    pair = slots // 4
    level = (s // 2) % 2
    base, far = level * 2 * pair + c * pair, (1 - level) * 2 * pair + c * pair
    partner, above, below = s + 1 - 2 * c, (s + 2) % ns, (s + ns - 2) % ns

    def along(a, b):
        return ((y + a * c + b * (1 - c)) % ny) * nx + (x + a * (1 - c) + b * c) % nx

    def table(j, first, count=pair):
        return cv_ref.at[j, pl.ds(first, count)]

    def post(ref, j, kind, to_s, to_m):
        send(ref, ref, c_send, c_recv.at[kind, j], to_s, to_m)

    def await_table(a, b):
        j = along(a, b)
        arrived(table(j, base), c_recv.at[0, j])
        return j

    def share(j):
        post(table(j, base, pair // 2), j, 1, above, m)
        post(table(j, base + pair // 2, pair // 2), j, 1, below, m)
        send(table(j, base), table(j, base), c_send, p_recv, partner, m)

    def both_ways(j):
        post(table(j, base), j, 0, s, along(0, 1))
        post(table(j, base), j, 0, s, along(0, nx - 1))

    def fan_first():
        post(table(m, base), m, 0, s, along(1, 0))
        post(table(m, base), m, 0, s, along(nx - 1, 0))
        both_ways(m)

    def pass_first(i, _):
        j = await_table(nx - 1 - 2 * i, 0)
        post(table(j, base + i * (pair // 2), pair // 2), j, 0, s, along(1 + 2 * i, 0))
        both_ways(j)
        share(j)
        return 0

    def pass_second(a, i):
        j = await_table(a, nx - 1 - 2 * i)
        post(table(j, base + i * (pair // 2), pair // 2), j, 0, s, along(0, 1 + 2 * i))
        share(j)

    def tables_one():
        lax.fori_loop(0, 2, pass_first, 0)

        def one(i, _):
            pass_second(0, i)
            return 0

        lax.fori_loop(0, 2, one, 0)

    def tables_two():
        j = await_table(2, 0)
        both_ways(j)
        share(j)

        def one(a, _):
            def each(i, _):
                pass_second(nx - 1 - 2 * a, i)
                return 0

            lax.fori_loop(0, 2, each, 0)
            return 0

        lax.fori_loop(0, 2, one, 0)

    def tables_three():
        def one(i, _):
            pass_second(2, i)
            return 0

        lax.fori_loop(0, 2, one, 0)

        def last(a, _):
            share(await_table(a, 2))
            return 0

        lax.fori_loop(0, nx, last, 0)

    def tables_other():
        def level_in(k, _):
            j = (m + k) % nm
            arrived(table(j, far), c_recv.at[1, j])
            send(table(j, far), table(j, far), c_send, p_recv, partner, m)
            return 0

        lax.fori_loop(1, nm, level_in, 0)
        arrived(cv_ref.at[pl.ds(0, nm - 1), pl.ds(0, 2 * pair)], p_recv)

    ghosts_out(0)
    loads[2].wait()
    fan_first()
    spread(A_F)
    loads[4].wait()
    loads[5].wait()
    ghosts_in(0)
    sf = part + dot(sg_ref[...], ghost_ref[0, :, 0:width])
    g_high, g_low = split(force_ref[...] - sf)
    sf_bf = sf.astype(BF)
    both = jnp.concatenate([g_high, sf_bf], axis=1)
    gsend_ref[1] = dot(oh_ref[...], both).astype(BF)
    ghosts_out(1)
    arr_ref[A_SF] = sf_bf
    arr_ref[A_G] = g_high
    arr_ref[A_GLO] = g_low
    tables_one()
    spread(A_SF)
    spread(A_G)
    spread(A_GLO)
    part = dot(sd_ref[...], both)
    ghosts_in(1)
    two = (part + dot(sg_ref[...], ghost_ref[1])).astype(BF)
    sg_bf = two[:, 0:width]
    gsend_ref[2, :, 0:width] = dot(oh_ref[...], sg_bf).astype(BF)
    ghosts_out(2)
    arr_ref[A_SG] = sg_bf
    arr_ref[A_S2F] = two[:, width : 2 * width]
    spread(A_SG)
    spread(A_S2F)
    tables_two()
    part = dot(sd_ref[...], sg_bf)
    ghosts_in(2)
    arr_ref[A_S2G] = (part + dot(sg_ref[...], ghost_ref[2, :, 0:width])).astype(BF)
    spread(A_S2G)
    tables_three()

    blocks = target_ref.shape[1]
    lane = lax.broadcasted_iota(jnp.int32, (blocks, blocks), 1)
    goal = lax.broadcasted_iota(jnp.int32, (blocks, blocks), 0)
    used = jnp.zeros((blocks, blocks), jnp.int32)
    for j in range(blocks):
        used = jnp.where(lane == j, count_ref[j], used)
    found = jnp.full((blocks, blocks), slots, jnp.int32)
    for q in range(slots):
        found = jnp.where((target_ref[q : q + 1, :] == goal) & (used > q), q, found)
    slot_ref[...] = jnp.zeros((blocks, 128), jnp.int32)
    slot_ref[:, 0:blocks] = found
    table_copy = pltpu.make_async_copy(slot_ref, inv_ref, l_sem.at[7])
    table_copy.start()

    lanes = 4 * slab

    def gather(buf):
        arrived(got_ref.at[buf, pl.ds(0, nm - 1), pl.ds(0, (3 + buf) * slab), :], a_recv.at[buf])

    def turn_x(j, _):
        rows = pl.ds(pl.multiple_of(j * width, width), width)
        x_ref[0, rows, 0:lanes] = (-jnp.transpose(got_ref[0, j].astype(F32))).astype(BF)
        x_ref[0, rows, lanes : 2 * lanes] = jnp.zeros((width, lanes), BF)
        return 0

    def turn_g(j, _):
        rows = pl.ds(pl.multiple_of(j * width, width), width)
        gt = jnp.transpose(got_ref[1, j].astype(F32))
        at = lax.broadcasted_iota(jnp.int32, (width, lanes), 1)
        add_ref[0, rows, :] = gt + jnp.where(at < slab, pltpu.roll(gt, slab, 1), 0.0)
        return 0

    gather(0)
    lax.fori_loop(0, nm, turn_x, 0)
    gather(1)
    lax.fori_loop(0, nm, turn_g, 0)
    tables_other()
    table_copy.wait()

    def build(t, _):
        for j in range(nm):
            w_ref[0, pl.ds(pl.multiple_of(t * width, width), width), j * width : (j + 1) * width] = cv_ref[j, inv_ref[t, j]]
        return 0

    lax.fori_loop(0, nm, build, 0)
    loads[6].wait()

    rows_at_once = nm * width // 2

    def apply(p, _):
        odd = p % 2

        def some(q, _):
            base = pl.multiple_of(q * rows_at_once, rows_at_once)
            rows = pl.ds(base, rows_at_once)
            prod = dot(w_ref[odd, rows, :], x_ref[odd])
            value = add_ref[odd, rows, :] + prod[:, 0:lanes] + prod[:, lanes:]
            high, low = split(value)
            x_ref[1 - odd, rows, 0:lanes] = high
            x_ref[1 - odd, rows, lanes:] = low
            add_ref[2 - 2 * odd, rows, :] = pltpu.roll(value, lanes - slab, 1)
            return 0

        lax.fori_loop(0, 2, some, 0)

        @pl.when(odd == 1)
        def _():
            def turn_back(i, _):
                at = lax.broadcasted_iota(jnp.int32, (width, lanes), 1)
                packed = add_ref[0, pl.ds(pl.multiple_of((4 * i + 3) * width, width), width), :]
                for g in range(3):
                    block = add_ref[0, pl.ds(pl.multiple_of((4 * i + g) * width, width), width), :]
                    packed = jnp.where((at >= g * slab) & (at < (g + 1) * slab), pltpu.roll(block, (g + 1) * slab, 1), packed)
                turned = jnp.transpose(packed)
                for g in range(4):
                    back_src[p // 2, 4 * i + g] = turned[g * slab : (g + 1) * slab, :]
                return 0

            lax.fori_loop(0, nm // 4, turn_back, 0, unroll=2)

        @pl.when((p == 1) | (p == 3))
        def _():
            back_out(p // 2)

        return 0

    def back_dst(a, many, one):
        return one if isinstance(a, int) and a == STEPS - 1 else many.at[a]

    def back_out(k):
        src, dst = back_dst(k, back_src, last_src), back_dst(k, back_got, last_got)

        def out(i, _):
            to = (m + i) % nm
            send(src.at[to], dst.at[m], b_send.at[k], b_recv.at[k], s, to)
            return 0

        lax.fori_loop(1, nm, out, 0)
        dst[m] = src[m]

    lax.fori_loop(0, 2 * STEPS, apply, 0)

    def line(a, b):
        return jnp.sum(back_src[a] * back_src[b], axis=(0, 1))[None, :]

    pairs = ((0, 0), (0, 1), (1, 1), (0, 2), (1, 2), (2, 2))
    gram = jnp.concatenate([line(a, b) for a, b in pairs] + [jnp.zeros((2, width), F32)], axis=0)
    gram_src[0] = gram
    gram_got[0, m] = gram

    def reduce_mode(k, _):
        to = (m + k) % nm
        send(gram_src.at[0], gram_got.at[0, m], r_send.at[0], r_recv.at[0], s, to)
        return 0

    lax.fori_loop(1, nm, reduce_mode, 0)
    last_src[...] = back_src[STEPS - 1].astype(BF)
    back_out(STEPS - 1)

    arrived(gram_got.at[0, pl.ds(0, nm - 1)], r_recv.at[0])
    gram = jnp.sum(gram_got[0, 0:nm], axis=0)
    gram_src[1] = gram
    gram_got[1, s] = gram

    def reduce_space(k, _):
        to = (s + k) % ns
        send(gram_src.at[1], gram_got.at[1, s], r_send.at[1], r_recv.at[1], to, m)
        return 0

    lax.fori_loop(1, ns, reduce_space, 0)

    for a in range(STEPS):
        arrived(back_dst(a, back_got, last_got).at[pl.ds(0, nm - 1)], b_recv.at[a])

    arrived(gram_got.at[1, pl.ds(0, ns - 1)], r_recv.at[1])
    total = jnp.sum(jnp.sum(gram_got[1, 0:ns], axis=0), axis=1, keepdims=True) * (1.0 / (nodes * ns * nm * width))
    g00, g01, g11, g02, g12, g22 = [total[r : r + 1, :] for r in range(6)]

    def damp(mean_square):
        return step_gain / jnp.sqrt(jnp.maximum(mean_square, 0.0) + 1e-06)

    d0 = damp(g00)
    d1 = damp(g00 - 2.0 * d0 * g01 + d0 * d0 * g11)
    p, q = -(d0 + d1), d0 * d1
    d2 = damp(g00 + p * p * g11 + q * q * g22 + 2.0 * (p * g01 + q * g02 + p * q * g12))
    a0 = d0 + d1 + d2
    a1 = -d0 * d1 - d2 * (d0 + d1)
    a2 = q * d2
    o_ref[...] = a0 * back_got[0] + a1 * back_got[1] + a2 * last_got[...].astype(F32)

    for r in range(3):
        ghosts_sent(r)

    sent(arr_ref.at[:, pl.ds(0, (nm - 1) * slab), :], a_send)
    sent(cv_ref.at[pl.ds(0, nm - 1), pl.ds(0, slots)], c_send)
    for a in range(STEPS):
        sent(back_dst(a, back_src, last_src).at[pl.ds(0, nm - 1)], b_send.at[a])
    sent(gram_got.at[0, pl.ds(0, nm - 1)], r_send.at[0])
    sent(gram_got.at[1, pl.ds(0, ns - 1)], r_send.at[1])


def solution(mesh):
    ns, nm = mesh.shape["space"], mesh.shape["mode"]
    nx = int(round(nm ** 0.5))

    def step(guess, forcing, spatial_diag, spatial_ghost, ghost_rows, chaos_vals, chaos_targets, chaos_count, mean_inverse):
        nodes, width = guess.shape
        ghost = ghost_rows.shape[1]
        blocks, slots = chaos_targets.shape
        modes = blocks * width
        slab = nodes // nm
        lanes = 4 * slab
        vmem = pl.BlockSpec(memory_space=pltpu.VMEM)
        dma = pltpu.SemaphoreType.DMA
        smem, anywhere = pl.BlockSpec(memory_space=pltpu.SMEM), pl.BlockSpec(memory_space=pl.ANY)
        gathered = pl.pallas_call(
            functools.partial(kernel, (ns, nm, nx, slab, ghost, width, slots)),
            out_shape=jax.ShapeDtypeStruct((nm, slab, width), F32),
            in_specs=[anywhere] * 6 + [vmem, smem, anywhere],
            out_specs=vmem,
            scratch_shapes=[
                pltpu.VMEM((nodes, width), F32),
                pltpu.VMEM((nodes, width), F32),
                pltpu.VMEM((nodes, nodes), BF),
                pltpu.VMEM((nodes, 2 * ghost), BF),
                pltpu.VMEM((2, ghost), jnp.int32),
                pltpu.VMEM((2, modes, modes), BF),
                pltpu.VMEM((nm, slots + 1, width, width), BF),
                pltpu.VMEM((blocks, 128), jnp.int32),
                pltpu.SMEM((blocks, 128), jnp.int32),
                pltpu.VMEM((2 * ghost, nodes), BF),
                pltpu.VMEM((7, nodes, width), BF),
                pltpu.VMEM((3, 2 * ghost, 2 * width), BF),
                pltpu.VMEM((3, 2 * ghost, 2 * width), BF),
                pltpu.VMEM((2, nm, lanes, width), BF),
                pltpu.VMEM((2, modes, 2 * lanes), BF),
                pltpu.VMEM((3, modes, lanes), F32),
                pltpu.VMEM((STEPS, nm, slab, width), F32),
                pltpu.VMEM((STEPS - 1, nm, slab, width), F32),
                pltpu.VMEM((nm, slab, width), BF),
                pltpu.VMEM((nm, slab, width), BF),
                pltpu.VMEM((2, 8, width), F32),
                pltpu.VMEM((2, max(nm, ns), 8, width), F32),
                dma((8,)),
                dma((3, 2)), dma((3, 2)),
                dma, dma((2,)),
                dma, dma((2, nm)), dma,
                dma((STEPS,)), dma((STEPS,)),
                dma((2,)), dma((2,)),
            ],
            compiler_params=pltpu.CompilerParams(
                collective_id=0, has_side_effects=True, vmem_limit_bytes=60 * 2**20
            ),
            name="galerkin",
        )(guess, forcing, spatial_diag, spatial_ghost, ghost_rows, chaos_vals, chaos_targets.T, chaos_count, mean_inverse)
        return guess + gathered.reshape(nodes, width)

    space, mode = P("space", "mode"), P("space", None)
    return jax.shard_map(
        step,
        mesh=mesh,
        in_specs=(space, space, mode, mode, mode, P("mode", None, None), P(), P(), P()),
        out_specs=space,
        check_vma=False,
    )
```

```python
import functools

import jax
import jax.numpy as jnp
from jax import lax
from jax.experimental import pallas as pl
from jax.experimental.pallas import tpu as pltpu
from jax.sharding import PartitionSpec as P

STEPS = 3
step_gain = 0.5
BF = jnp.bfloat16
F32 = jnp.float32
A_F, A_SF, A_G, A_GLO, A_SG, A_S2F, A_S2G = range(7)
PLACE = {A_F: (0, 0), A_SF: (0, 1), A_S2F: (0, 2), A_G: (1, 0), A_SG: (1, 1), A_S2G: (1, 2), A_GLO: (1, 3)}


def dot(a, b):
    return jnp.dot(a, b, preferred_element_type=F32)


def split(x):
    high = x.astype(BF)
    return high, (x - high.astype(F32)).astype(BF)


def kernel(
    sizes,
    f_hbm, force_hbm, sd_hbm, sg_hbm, rows_hbm, vals_hbm, target_ref, count_ref, m_hbm,
    o_ref,
    f_ref, force_ref, sd_ref, sg_ref, rows_ref,
    w_ref, cv_ref, slot_ref, inv_ref, oh_ref, arr_ref, gsend_ref, ghost_ref,
    got_ref, x_ref, add_ref, back_src, back_got, last_src, last_got, gram_src, gram_got,
    l_sem, gh_send, gh_recv, a_send, a_recv, c_send, c_recv, p_recv, b_send, b_recv, r_send, r_recv,
):
    ns, nm, nx, slab, ghost, width, slots = sizes
    ny = nm // nx
    nodes = f_ref.shape[0]
    s, m = lax.axis_index("space"), lax.axis_index("mode")
    c = s % 2
    y, x = m // nx, m % nx
    mesh = pl.DeviceIdType.MESH

    def send(src, dst, ssem, rsem, to_s, to_m):
        cp = pltpu.make_async_remote_copy(
            src_ref=src, dst_ref=dst, send_sem=ssem, recv_sem=rsem,
            device_id={"space": to_s, "mode": to_m}, device_id_type=mesh,
        )
        cp.start()

    def arrived(dst, rsem):
        pltpu.make_async_remote_copy(
            src_ref=dst, dst_ref=dst, send_sem=rsem, recv_sem=rsem,
            device_id={"space": s, "mode": m}, device_id_type=mesh,
        ).wait_recv()

    def sent(src, ssem):
        pltpu.make_async_remote_copy(
            src_ref=src, dst_ref=src, send_sem=ssem, recv_sem=ssem,
            device_id={"space": s, "mode": m}, device_id_type=mesh,
        ).wait_send()

    barrier = pltpu.get_barrier_semaphore()

    def greet_mode(k, _):
        pl.semaphore_signal(barrier, inc=1, device_id={"space": s, "mode": (m + k) % nm}, device_id_type=mesh)
        return 0

    def greet_space(k, _):
        pl.semaphore_signal(barrier, inc=1, device_id={"space": (s + k) % ns, "mode": m}, device_id_type=mesh)
        return 0

    lax.fori_loop(1, nm, greet_mode, 0)
    lax.fori_loop(1, ns, greet_space, 0)

    loads = [
        pltpu.make_async_copy(src, dst, l_sem.at[n])
        for n, (src, dst) in enumerate((
            (f_hbm, f_ref), (rows_hbm, rows_ref), (vals_hbm, cv_ref.at[m, pl.ds(0, slots)]),
            (sd_hbm, sd_ref), (sg_hbm, sg_ref), (force_hbm, force_ref), (m_hbm, w_ref.at[1]),
        ))
    ]
    for load in loads:
        load.start()
    loads[0].wait()
    loads[1].wait()

    f_bf = f_ref[...].astype(BF)
    arr_ref[A_F] = f_bf
    for side in range(2):
        hits = lax.broadcasted_iota(jnp.int32, (nodes, ghost), 0) == rows_ref[side : side + 1, :]
        picks = jnp.transpose(jnp.where(hits, 1.0, 0.0).astype(F32))
        oh_ref[side * ghost : (side + 1) * ghost, :] = picks.astype(BF)
    picked = dot(oh_ref[...], f_bf).astype(BF)
    gsend_ref[0, :, 0:width] = picked

    def zero_tail(j, _):
        cv_ref[j, slots] = jnp.zeros((width, width), BF)
        got_ref[0, j, pl.ds(3 * slab, slab), :] = jnp.zeros((slab, width), BF)
        add_ref[1, pl.ds(pl.multiple_of(j * width, width), width), :] = jnp.zeros((width, 4 * slab), F32)
        return 0

    lax.fori_loop(0, nm, zero_tail, 0)

    @pl.when(s == 0)
    def _():
        for r in range(3):
            ghost_ref[r, 0:ghost, :] = jnp.zeros((ghost, 2 * width), BF)

    @pl.when(s == ns - 1)
    def _():
        for r in range(3):
            ghost_ref[r, ghost : 2 * ghost, :] = jnp.zeros((ghost, 2 * width), BF)

    loads[3].wait()
    part = dot(sd_ref[...], f_bf)
    pl.semaphore_wait(barrier, nm - 1 + ns - 1)

    wide = [width, 2 * width, width]

    def ghosts_out(r):
        w = wide[r]

        @pl.when(s > 0)
        def _():
            send(gsend_ref.at[r, pl.ds(0, ghost), pl.ds(0, w)], ghost_ref.at[r, pl.ds(ghost, ghost), pl.ds(0, w)],
                 gh_send.at[r, 0], gh_recv.at[r, 1], s - 1, m)

        @pl.when(s < ns - 1)
        def _():
            send(gsend_ref.at[r, pl.ds(ghost, ghost), pl.ds(0, w)], ghost_ref.at[r, pl.ds(0, ghost), pl.ds(0, w)],
                 gh_send.at[r, 1], gh_recv.at[r, 0], s + 1, m)

    def ghosts_in(r):
        w = wide[r]

        @pl.when(s > 0)
        def _():
            arrived(ghost_ref.at[r, pl.ds(0, ghost), pl.ds(0, w)], gh_recv.at[r, 0])

        @pl.when(s < ns - 1)
        def _():
            arrived(ghost_ref.at[r, pl.ds(ghost, ghost), pl.ds(0, w)], gh_recv.at[r, 1])

    def ghosts_sent(r):
        w = wide[r]

        @pl.when(s > 0)
        def _():
            sent(gsend_ref.at[r, pl.ds(0, ghost), pl.ds(0, w)], gh_send.at[r, 0])

        @pl.when(s < ns - 1)
        def _():
            sent(gsend_ref.at[r, pl.ds(ghost, ghost), pl.ds(0, w)], gh_send.at[r, 1])

    def spread(a):
        buf, row = PLACE[a]

        def one(k, _):
            to = (m + k) % nm
            send(arr_ref.at[a, pl.ds(to * slab, slab), :], got_ref.at[buf, m, pl.ds(row * slab, slab), :],
                 a_send, a_recv.at[buf], s, to)
            return 0

        lax.fori_loop(1, nm, one, 0)
        got_ref[buf, m, pl.ds(row * slab, slab), :] = arr_ref[a, pl.ds(m * slab, slab), :]

    pair = slots // 4
    level = (s // 2) % 2
    base, far = level * 2 * pair + c * pair, (1 - level) * 2 * pair + c * pair
    partner, above, below = s + 1 - 2 * c, (s + 2) % ns, (s + ns - 2) % ns

    def along(a, b):
        return ((y + a * c + b * (1 - c)) % ny) * nx + (x + a * (1 - c) + b * c) % nx

    def table(j, first, count=pair):
        return cv_ref.at[j, pl.ds(first, count)]

    def post(ref, j, kind, to_s, to_m):
        send(ref, ref, c_send, c_recv.at[kind, j], to_s, to_m)

    def await_table(a, b):
        j = along(a, b)
        arrived(table(j, base), c_recv.at[0, j])
        return j

    def share(j):
        post(table(j, base, pair // 2), j, 1, above, m)
        post(table(j, base + pair // 2, pair // 2), j, 1, below, m)
        send(table(j, base), table(j, base), c_send, p_recv, partner, m)

    def both_ways(j):
        post(table(j, base), j, 0, s, along(0, 1))
        post(table(j, base), j, 0, s, along(0, nx - 1))

    def fan_first():
        post(table(m, base), m, 0, s, along(1, 0))
        post(table(m, base), m, 0, s, along(nx - 1, 0))
        post(table(m, base), m, 0, s, along(2, 0))
        both_ways(m)

    def pass_first(a, _):
        j = await_table(a, 0)
        both_ways(j)
        share(j)
        return 0

    def pass_second(a, i):
        j = await_table(a, nx - 1 - 2 * i)
        post(table(j, base + i * (pair // 2), pair // 2), j, 0, s, along(0, 1 + 2 * i))
        share(j)

    def tables_one():
        lax.fori_loop(1, nx, pass_first, 0)

        def one(i, _):
            pass_second(0, i)
            return 0

        lax.fori_loop(0, 2, one, 0)

    def tables_two():
        def one(a, _):
            def each(i, _):
                pass_second(a, i)
                return 0

            lax.fori_loop(0, 2, each, 0)
            return 0

        lax.fori_loop(1, nx, one, 0)

    def tables_three():
        def last(a, _):
            share(await_table(a, 2))
            return 0

        lax.fori_loop(0, nx, last, 0)

    def tables_other():
        def level_in(k, _):
            j = (m + k) % nm
            arrived(table(j, far), c_recv.at[1, j])
            send(table(j, far), table(j, far), c_send, p_recv, partner, m)
            return 0

        lax.fori_loop(1, nm, level_in, 0)

    ghosts_out(0)
    loads[2].wait()
    fan_first()
    spread(A_F)
    loads[4].wait()
    loads[5].wait()
    ghosts_in(0)
    sf = part + dot(sg_ref[...], ghost_ref[0, :, 0:width])
    g_high, g_low = split(force_ref[...] - sf)
    sf_bf = sf.astype(BF)
    both = jnp.concatenate([g_high, sf_bf], axis=1)
    gsend_ref[1] = dot(oh_ref[...], both).astype(BF)
    ghosts_out(1)
    arr_ref[A_SF] = sf_bf
    arr_ref[A_G] = g_high
    arr_ref[A_GLO] = g_low
    tables_one()
    spread(A_SF)
    spread(A_G)
    spread(A_GLO)
    part = dot(sd_ref[...], both)
    ghosts_in(1)
    two = (part + dot(sg_ref[...], ghost_ref[1])).astype(BF)
    sg_bf = two[:, 0:width]
    gsend_ref[2, :, 0:width] = dot(oh_ref[...], sg_bf).astype(BF)
    ghosts_out(2)
    arr_ref[A_SG] = sg_bf
    arr_ref[A_S2F] = two[:, width : 2 * width]
    tables_two()
    spread(A_SG)
    spread(A_S2F)
    part = dot(sd_ref[...], sg_bf)
    ghosts_in(2)
    arr_ref[A_S2G] = (part + dot(sg_ref[...], ghost_ref[2, :, 0:width])).astype(BF)
    spread(A_S2G)
    tables_three()

    blocks = target_ref.shape[1]
    lane = lax.broadcasted_iota(jnp.int32, (blocks, blocks), 1)
    goal = lax.broadcasted_iota(jnp.int32, (blocks, blocks), 0)
    used = jnp.zeros((blocks, blocks), jnp.int32)
    for j in range(blocks):
        used = jnp.where(lane == j, count_ref[j], used)
    found = jnp.full((blocks, blocks), slots, jnp.int32)
    for q in range(slots):
        found = jnp.where((target_ref[q : q + 1, :] == goal) & (used > q), q, found)
    slot_ref[...] = jnp.zeros((blocks, 128), jnp.int32)
    slot_ref[:, 0:blocks] = found
    table_copy = pltpu.make_async_copy(slot_ref, inv_ref, l_sem.at[7])
    table_copy.start()

    lanes = 4 * slab

    def gather(buf):
        arrived(got_ref.at[buf, pl.ds(0, nm - 1), pl.ds(0, (3 + buf) * slab), :], a_recv.at[buf])

    def turn_x(j, _):
        rows = pl.ds(pl.multiple_of(j * width, width), width)
        x_ref[0, rows, 0:lanes] = (-jnp.transpose(got_ref[0, j].astype(F32))).astype(BF)
        x_ref[0, rows, lanes : 2 * lanes] = jnp.zeros((width, lanes), BF)
        return 0

    def turn_g(j, _):
        rows = pl.ds(pl.multiple_of(j * width, width), width)
        gt = jnp.transpose(got_ref[1, j].astype(F32))
        at = lax.broadcasted_iota(jnp.int32, (width, lanes), 1)
        add_ref[0, rows, :] = gt + jnp.where(at < slab, pltpu.roll(gt, slab, 1), 0.0)
        return 0

    gather(0)
    lax.fori_loop(0, nm, turn_x, 0)
    tables_other()
    gather(1)
    lax.fori_loop(0, nm, turn_g, 0)
    arrived(cv_ref.at[pl.ds(0, nm - 1), pl.ds(0, 2 * pair)], p_recv)
    table_copy.wait()

    def build(t, _):
        for j in range(nm):
            w_ref[0, pl.ds(pl.multiple_of(t * width, width), width), j * width : (j + 1) * width] = cv_ref[j, inv_ref[t, j]]
        return 0

    lax.fori_loop(0, nm, build, 0)
    loads[6].wait()

    rows_at_once = nm * width // 2

    def apply(p, _):
        odd = p % 2

        def some(q, _):
            base = pl.multiple_of(q * rows_at_once, rows_at_once)
            rows = pl.ds(base, rows_at_once)
            prod = dot(w_ref[odd, rows, :], x_ref[odd])
            value = add_ref[odd, rows, :] + prod[:, 0:lanes] + prod[:, lanes:]
            high, low = split(value)
            x_ref[1 - odd, rows, 0:lanes] = high
            x_ref[1 - odd, rows, lanes:] = low
            add_ref[2 - 2 * odd, rows, :] = pltpu.roll(value, lanes - slab, 1)
            return 0

        lax.fori_loop(0, 2, some, 0)

        @pl.when(odd == 1)
        def _():
            def turn_back(i, _):
                at = lax.broadcasted_iota(jnp.int32, (width, lanes), 1)
                packed = add_ref[0, pl.ds(pl.multiple_of((4 * i + 3) * width, width), width), :]
                for g in range(3):
                    block = add_ref[0, pl.ds(pl.multiple_of((4 * i + g) * width, width), width), :]
                    packed = jnp.where((at >= g * slab) & (at < (g + 1) * slab), pltpu.roll(block, (g + 1) * slab, 1), packed)
                turned = jnp.transpose(packed)
                for g in range(4):
                    back_src[p // 2, 4 * i + g] = turned[g * slab : (g + 1) * slab, :]
                return 0

            lax.fori_loop(0, nm // 4, turn_back, 0, unroll=2)

        @pl.when((p == 1) | (p == 3))
        def _():
            back_out(p // 2)

        return 0

    def back_dst(a, many, one):
        return one if isinstance(a, int) and a == STEPS - 1 else many.at[a]

    def back_out(k):
        src, dst = back_dst(k, back_src, last_src), back_dst(k, back_got, last_got)

        def out(i, _):
            to = (m + i) % nm
            send(src.at[to], dst.at[m], b_send.at[k], b_recv.at[k], s, to)
            return 0

        lax.fori_loop(1, nm, out, 0)
        dst[m] = src[m]

    lax.fori_loop(0, 2 * STEPS, apply, 0)

    def line(a, b):
        return jnp.sum(back_src[a] * back_src[b], axis=(0, 1))[None, :]

    pairs = ((0, 0), (0, 1), (1, 1), (0, 2), (1, 2), (2, 2))
    gram = jnp.concatenate([line(a, b) for a, b in pairs] + [jnp.zeros((2, width), F32)], axis=0)
    gram_src[0] = gram
    gram_got[0, m] = gram

    def reduce_mode(k, _):
        to = (m + k) % nm
        send(gram_src.at[0], gram_got.at[0, m], r_send.at[0], r_recv.at[0], s, to)
        return 0

    lax.fori_loop(1, nm, reduce_mode, 0)
    last_src[...] = back_src[STEPS - 1].astype(BF)
    back_out(STEPS - 1)

    arrived(gram_got.at[0, pl.ds(0, nm - 1)], r_recv.at[0])
    gram = jnp.sum(gram_got[0, 0:nm], axis=0)
    gram_src[1] = gram
    gram_got[1, s] = gram

    def reduce_space(k, _):
        to = (s + k) % ns
        send(gram_src.at[1], gram_got.at[1, s], r_send.at[1], r_recv.at[1], to, m)
        return 0

    lax.fori_loop(1, ns, reduce_space, 0)

    for a in range(STEPS):
        arrived(back_dst(a, back_got, last_got).at[pl.ds(0, nm - 1)], b_recv.at[a])

    arrived(gram_got.at[1, pl.ds(0, ns - 1)], r_recv.at[1])
    total = jnp.sum(jnp.sum(gram_got[1, 0:ns], axis=0), axis=1, keepdims=True) * (1.0 / (nodes * ns * nm * width))
    g00, g01, g11, g02, g12, g22 = [total[r : r + 1, :] for r in range(6)]

    def damp(mean_square):
        return step_gain / jnp.sqrt(jnp.maximum(mean_square, 0.0) + 1e-06)

    d0 = damp(g00)
    d1 = damp(g00 - 2.0 * d0 * g01 + d0 * d0 * g11)
    p, q = -(d0 + d1), d0 * d1
    d2 = damp(g00 + p * p * g11 + q * q * g22 + 2.0 * (p * g01 + q * g02 + p * q * g12))
    a0 = d0 + d1 + d2
    a1 = -d0 * d1 - d2 * (d0 + d1)
    a2 = q * d2
    o_ref[...] = a0 * back_got[0] + a1 * back_got[1] + a2 * last_got[...].astype(F32)

    for r in range(3):
        ghosts_sent(r)

    sent(arr_ref.at[:, pl.ds(0, (nm - 1) * slab), :], a_send)
    sent(cv_ref.at[pl.ds(0, nm - 1), pl.ds(0, slots)], c_send)
    for a in range(STEPS):
        sent(back_dst(a, back_src, last_src).at[pl.ds(0, nm - 1)], b_send.at[a])
    sent(gram_got.at[0, pl.ds(0, nm - 1)], r_send.at[0])
    sent(gram_got.at[1, pl.ds(0, ns - 1)], r_send.at[1])


def solution(mesh):
    ns, nm = mesh.shape["space"], mesh.shape["mode"]
    nx = int(round(nm ** 0.5))

    def step(guess, forcing, spatial_diag, spatial_ghost, ghost_rows, chaos_vals, chaos_targets, chaos_count, mean_inverse):
        nodes, width = guess.shape
        ghost = ghost_rows.shape[1]
        blocks, slots = chaos_targets.shape
        modes = blocks * width
        slab = nodes // nm
        lanes = 4 * slab
        vmem = pl.BlockSpec(memory_space=pltpu.VMEM)
        dma = pltpu.SemaphoreType.DMA
        smem, anywhere = pl.BlockSpec(memory_space=pltpu.SMEM), pl.BlockSpec(memory_space=pl.ANY)
        gathered = pl.pallas_call(
            functools.partial(kernel, (ns, nm, nx, slab, ghost, width, slots)),
            out_shape=jax.ShapeDtypeStruct((nm, slab, width), F32),
            in_specs=[anywhere] * 6 + [vmem, smem, anywhere],
            out_specs=vmem,
            scratch_shapes=[
                pltpu.VMEM((nodes, width), F32),
                pltpu.VMEM((nodes, width), F32),
                pltpu.VMEM((nodes, nodes), BF),
                pltpu.VMEM((nodes, 2 * ghost), BF),
                pltpu.VMEM((2, ghost), jnp.int32),
                pltpu.VMEM((2, modes, modes), BF),
                pltpu.VMEM((nm, slots + 1, width, width), BF),
                pltpu.VMEM((blocks, 128), jnp.int32),
                pltpu.SMEM((blocks, 128), jnp.int32),
                pltpu.VMEM((2 * ghost, nodes), BF),
                pltpu.VMEM((7, nodes, width), BF),
                pltpu.VMEM((3, 2 * ghost, 2 * width), BF),
                pltpu.VMEM((3, 2 * ghost, 2 * width), BF),
                pltpu.VMEM((2, nm, lanes, width), BF),
                pltpu.VMEM((2, modes, 2 * lanes), BF),
                pltpu.VMEM((3, modes, lanes), F32),
                pltpu.VMEM((STEPS, nm, slab, width), F32),
                pltpu.VMEM((STEPS - 1, nm, slab, width), F32),
                pltpu.VMEM((nm, slab, width), BF),
                pltpu.VMEM((nm, slab, width), BF),
                pltpu.VMEM((2, 8, width), F32),
                pltpu.VMEM((2, max(nm, ns), 8, width), F32),
                dma((8,)),
                dma((3, 2)), dma((3, 2)),
                dma, dma((2,)),
                dma, dma((2, nm)), dma,
                dma((STEPS,)), dma((STEPS,)),
                dma((2,)), dma((2,)),
            ],
            compiler_params=pltpu.CompilerParams(
                collective_id=0, has_side_effects=True, vmem_limit_bytes=60 * 2**20
            ),
            name="galerkin",
        )(guess, forcing, spatial_diag, spatial_ghost, ghost_rows, chaos_vals, chaos_targets.T, chaos_count, mean_inverse)
        return guess + gathered.reshape(nodes, width)

    space, mode = P("space", "mode"), P("space", None)
    return jax.shard_map(
        step,
        mesh=mesh,
        in_specs=(space, space, mode, mode, mode, P("mode", None, None), P(), P(), P()),
        out_specs=space,
        check_vma=False,
    )
```

```python
import functools

import jax
import jax.numpy as jnp
from jax import lax
from jax.experimental import pallas as pl
from jax.experimental.pallas import tpu as pltpu
from jax.sharding import PartitionSpec as P

STEPS = 3
step_gain = 0.5
BF = jnp.bfloat16
F32 = jnp.float32
A_F, A_SF, A_G, A_GLO, A_SG, A_S2F, A_S2G = range(7)
PLACE = {A_F: (0, 0), A_SF: (0, 1), A_S2F: (0, 2), A_G: (1, 0), A_SG: (1, 1), A_S2G: (1, 2), A_GLO: (1, 3)}


def dot(a, b):
    return jnp.dot(a, b, preferred_element_type=F32)


def split(x):
    high = x.astype(BF)
    return high, (x - high.astype(F32)).astype(BF)


def kernel(
    sizes,
    f_hbm, force_hbm, sd_hbm, sg_hbm, rows_hbm, vals_hbm, target_ref, count_ref, m_hbm,
    o_ref,
    f_ref, force_ref, sd_ref, sg_ref, rows_ref,
    w_ref, cv_ref, slot_ref, inv_ref, oh_ref, arr_ref, gsend_ref, ghost_ref,
    got_ref, x_ref, add_ref, back_src, back_got, last_src, last_got, gram_src, gram_got,
    l_sem, gh_send, gh_recv, a_send, a_recv, c_send, c_recv, p_recv, b_send, b_recv, r_send, r_recv,
):
    ns, nm, nx, slab, ghost, width, slots = sizes
    ny = nm // nx
    nodes = f_ref.shape[0]
    s, m = lax.axis_index("space"), lax.axis_index("mode")
    c = s % 2
    y, x = m // nx, m % nx
    mesh = pl.DeviceIdType.MESH

    def send(src, dst, ssem, rsem, to_s, to_m):
        cp = pltpu.make_async_remote_copy(
            src_ref=src, dst_ref=dst, send_sem=ssem, recv_sem=rsem,
            device_id={"space": to_s, "mode": to_m}, device_id_type=mesh,
        )
        cp.start()

    def arrived(dst, rsem):
        pltpu.make_async_remote_copy(
            src_ref=dst, dst_ref=dst, send_sem=rsem, recv_sem=rsem,
            device_id={"space": s, "mode": m}, device_id_type=mesh,
        ).wait_recv()

    def sent(src, ssem):
        pltpu.make_async_remote_copy(
            src_ref=src, dst_ref=src, send_sem=ssem, recv_sem=ssem,
            device_id={"space": s, "mode": m}, device_id_type=mesh,
        ).wait_send()

    barrier = pltpu.get_barrier_semaphore()

    def greet_mode(k, _):
        pl.semaphore_signal(barrier, inc=1, device_id={"space": s, "mode": (m + k) % nm}, device_id_type=mesh)
        return 0

    def greet_space(k, _):
        pl.semaphore_signal(barrier, inc=1, device_id={"space": (s + k) % ns, "mode": m}, device_id_type=mesh)
        return 0

    lax.fori_loop(1, nm, greet_mode, 0)
    lax.fori_loop(1, ns, greet_space, 0)

    loads = [
        pltpu.make_async_copy(src, dst, l_sem.at[n])
        for n, (src, dst) in enumerate((
            (f_hbm, f_ref), (rows_hbm, rows_ref), (vals_hbm, cv_ref.at[m, pl.ds(0, slots)]),
            (sd_hbm, sd_ref), (sg_hbm, sg_ref), (force_hbm, force_ref), (m_hbm, w_ref.at[1]),
        ))
    ]
    for load in loads:
        load.start()
    loads[0].wait()
    loads[1].wait()

    f_bf = f_ref[...].astype(BF)
    arr_ref[A_F] = f_bf
    for side in range(2):
        hits = lax.broadcasted_iota(jnp.int32, (nodes, ghost), 0) == rows_ref[side : side + 1, :]
        picks = jnp.transpose(jnp.where(hits, 1.0, 0.0).astype(F32))
        oh_ref[side * ghost : (side + 1) * ghost, :] = picks.astype(BF)
    picked = dot(oh_ref[...], f_bf).astype(BF)
    gsend_ref[0, :, 0:width] = picked

    def zero_tail(j, _):
        cv_ref[j, slots] = jnp.zeros((width, width), BF)
        got_ref[0, j, pl.ds(3 * slab, slab), :] = jnp.zeros((slab, width), BF)
        add_ref[1, pl.ds(pl.multiple_of(j * width, width), width), :] = jnp.zeros((width, 4 * slab), F32)
        return 0

    lax.fori_loop(0, nm, zero_tail, 0)

    @pl.when(s == 0)
    def _():
        for r in range(3):
            ghost_ref[r, 0:ghost, :] = jnp.zeros((ghost, 2 * width), BF)

    @pl.when(s == ns - 1)
    def _():
        for r in range(3):
            ghost_ref[r, ghost : 2 * ghost, :] = jnp.zeros((ghost, 2 * width), BF)

    loads[3].wait()
    part = dot(sd_ref[...], f_bf)
    pl.semaphore_wait(barrier, nm - 1 + ns - 1)

    wide = [width, 2 * width, width]

    def ghosts_out(r):
        w = wide[r]

        @pl.when(s > 0)
        def _():
            send(gsend_ref.at[r, pl.ds(0, ghost), pl.ds(0, w)], ghost_ref.at[r, pl.ds(ghost, ghost), pl.ds(0, w)],
                 gh_send.at[r, 0], gh_recv.at[r, 1], s - 1, m)

        @pl.when(s < ns - 1)
        def _():
            send(gsend_ref.at[r, pl.ds(ghost, ghost), pl.ds(0, w)], ghost_ref.at[r, pl.ds(0, ghost), pl.ds(0, w)],
                 gh_send.at[r, 1], gh_recv.at[r, 0], s + 1, m)

    def ghosts_in(r):
        w = wide[r]

        @pl.when(s > 0)
        def _():
            arrived(ghost_ref.at[r, pl.ds(0, ghost), pl.ds(0, w)], gh_recv.at[r, 0])

        @pl.when(s < ns - 1)
        def _():
            arrived(ghost_ref.at[r, pl.ds(ghost, ghost), pl.ds(0, w)], gh_recv.at[r, 1])

    def ghosts_sent(r):
        w = wide[r]

        @pl.when(s > 0)
        def _():
            sent(gsend_ref.at[r, pl.ds(0, ghost), pl.ds(0, w)], gh_send.at[r, 0])

        @pl.when(s < ns - 1)
        def _():
            sent(gsend_ref.at[r, pl.ds(ghost, ghost), pl.ds(0, w)], gh_send.at[r, 1])

    def spread(a):
        buf, row = PLACE[a]

        def one(k, _):
            to = (m + k) % nm
            send(arr_ref.at[a, pl.ds(to * slab, slab), :], got_ref.at[buf, m, pl.ds(row * slab, slab), :],
                 a_send, a_recv.at[buf], s, to)
            return 0

        lax.fori_loop(1, nm, one, 0)
        got_ref[buf, m, pl.ds(row * slab, slab), :] = arr_ref[a, pl.ds(m * slab, slab), :]

    pair = slots // 4
    level = (s // 2) % 2
    base, far = level * 2 * pair + c * pair, (1 - level) * 2 * pair + c * pair
    partner, above, below = s + 1 - 2 * c, (s + 2) % ns, (s + ns - 2) % ns

    def along(a, b):
        return ((y + a * c + b * (1 - c)) % ny) * nx + (x + a * (1 - c) + b * c) % nx

    def table(j, first, count=pair):
        return cv_ref.at[j, pl.ds(first, count)]

    def post(ref, j, kind, to_s, to_m):
        send(ref, ref, c_send, c_recv.at[kind, j], to_s, to_m)

    def await_table(a, b):
        j = along(a, b)
        arrived(table(j, base), c_recv.at[0, j])
        return j

    def share(j):
        post(table(j, base, pair // 2), j, 1, above, m)
        post(table(j, base + pair // 2, pair // 2), j, 1, below, m)
        send(table(j, base), table(j, base), c_send, p_recv, partner, m)

    def both_ways(j):
        post(table(j, base), j, 0, s, along(0, 1))
        post(table(j, base), j, 0, s, along(0, nx - 1))

    def fan_first():
        post(table(m, base), m, 0, s, along(1, 0))
        post(table(m, base), m, 0, s, along(nx - 1, 0))
        post(table(m, base), m, 0, s, along(2, 0))
        both_ways(m)

    def pass_first(a, _):
        j = await_table(a, 0)
        both_ways(j)
        share(j)
        return 0

    def pass_second(a, i):
        j = await_table(a, nx - 1 - 2 * i)
        post(table(j, base + i * (pair // 2), pair // 2), j, 0, s, along(0, 1 + 2 * i))
        share(j)

    def tables_one():
        lax.fori_loop(1, nx, pass_first, 0)

        def one(i, _):
            pass_second(0, i)
            return 0

        lax.fori_loop(0, 2, one, 0)

    def tables_two():
        def one(a, _):
            def each(i, _):
                pass_second(a, i)
                return 0

            lax.fori_loop(0, 2, each, 0)
            return 0

        lax.fori_loop(1, nx, one, 0)

    def tables_three():
        def last(a, _):
            share(await_table(a, 2))
            return 0

        lax.fori_loop(0, nx, last, 0)

    def tables_other():
        def level_in(k, _):
            j = (m + k) % nm
            arrived(table(j, far), c_recv.at[1, j])
            send(table(j, far), table(j, far), c_send, p_recv, partner, m)
            return 0

        lax.fori_loop(1, nm, level_in, 0)

    ghosts_out(0)
    loads[2].wait()
    fan_first()
    spread(A_F)
    loads[4].wait()
    loads[5].wait()
    ghosts_in(0)
    sf = part + dot(sg_ref[...], ghost_ref[0, :, 0:width])
    g_high, g_low = split(force_ref[...] - sf)
    sf_bf = sf.astype(BF)
    both = jnp.concatenate([g_high, sf_bf], axis=1)
    gsend_ref[1] = dot(oh_ref[...], both).astype(BF)
    ghosts_out(1)
    arr_ref[A_SF] = sf_bf
    arr_ref[A_G] = g_high
    arr_ref[A_GLO] = g_low
    tables_one()
    spread(A_SF)
    spread(A_G)
    spread(A_GLO)
    part = dot(sd_ref[...], both)
    ghosts_in(1)
    two = (part + dot(sg_ref[...], ghost_ref[1])).astype(BF)
    sg_bf = two[:, 0:width]
    gsend_ref[2, :, 0:width] = dot(oh_ref[...], sg_bf).astype(BF)
    ghosts_out(2)
    arr_ref[A_SG] = sg_bf
    arr_ref[A_S2F] = two[:, width : 2 * width]
    tables_two()
    spread(A_SG)
    spread(A_S2F)
    part = dot(sd_ref[...], sg_bf)
    ghosts_in(2)
    arr_ref[A_S2G] = (part + dot(sg_ref[...], ghost_ref[2, :, 0:width])).astype(BF)
    spread(A_S2G)
    tables_three()

    blocks = target_ref.shape[1]
    lane = lax.broadcasted_iota(jnp.int32, (blocks, blocks), 1)
    goal = lax.broadcasted_iota(jnp.int32, (blocks, blocks), 0)
    used = jnp.zeros((blocks, blocks), jnp.int32)
    for j in range(blocks):
        used = jnp.where(lane == j, count_ref[j], used)
    found = jnp.full((blocks, blocks), slots, jnp.int32)
    for q in range(slots):
        found = jnp.where((target_ref[q : q + 1, :] == goal) & (used > q), q, found)
    slot_ref[...] = jnp.zeros((blocks, 128), jnp.int32)
    slot_ref[:, 0:blocks] = found
    table_copy = pltpu.make_async_copy(slot_ref, inv_ref, l_sem.at[7])
    table_copy.start()

    lanes = 4 * slab

    def gather(buf):
        arrived(got_ref.at[buf, pl.ds(0, nm - 1), pl.ds(0, (3 + buf) * slab), :], a_recv.at[buf])

    def turn_x(j, _):
        rows = pl.ds(pl.multiple_of(j * width, width), width)
        x_ref[0, rows, 0:lanes] = (-jnp.transpose(got_ref[0, j].astype(F32))).astype(BF)
        x_ref[0, rows, lanes : 2 * lanes] = jnp.zeros((width, lanes), BF)
        return 0

    def turn_g(j, _):
        rows = pl.ds(pl.multiple_of(j * width, width), width)
        gt = jnp.transpose(got_ref[1, j].astype(F32))
        at = lax.broadcasted_iota(jnp.int32, (width, lanes), 1)
        add_ref[0, rows, :] = gt + jnp.where(at < slab, pltpu.roll(gt, slab, 1), 0.0)
        return 0

    gather(0)
    lax.fori_loop(0, nm, turn_x, 0, unroll=4)
    tables_other()
    gather(1)
    lax.fori_loop(0, nm, turn_g, 0, unroll=4)
    arrived(cv_ref.at[pl.ds(0, nm - 1), pl.ds(0, 2 * pair)], p_recv)
    table_copy.wait()

    def build(t, _):
        for j in range(nm):
            w_ref[0, pl.ds(pl.multiple_of(t * width, width), width), j * width : (j + 1) * width] = cv_ref[j, inv_ref[t, j]]
        return 0

    lax.fori_loop(0, nm, build, 0, unroll=2)
    loads[6].wait()

    rows_at_once = nm * width // 2

    def apply(p, _):
        odd = p % 2

        def some(q, _):
            base = pl.multiple_of(q * rows_at_once, rows_at_once)
            rows = pl.ds(base, rows_at_once)
            prod = dot(w_ref[odd, rows, :], x_ref[odd])
            value = add_ref[odd, rows, :] + prod[:, 0:lanes] + prod[:, lanes:]
            high, low = split(value)
            x_ref[1 - odd, rows, 0:lanes] = high
            x_ref[1 - odd, rows, lanes:] = low
            add_ref[2 - 2 * odd, rows, :] = pltpu.roll(value, lanes - slab, 1)
            return 0

        lax.fori_loop(0, 2, some, 0)

        @pl.when(odd == 1)
        def _():
            def turn_back(i, _):
                at = lax.broadcasted_iota(jnp.int32, (width, lanes), 1)
                packed = add_ref[0, pl.ds(pl.multiple_of((4 * i + 3) * width, width), width), :]
                for g in range(3):
                    block = add_ref[0, pl.ds(pl.multiple_of((4 * i + g) * width, width), width), :]
                    packed = jnp.where((at >= g * slab) & (at < (g + 1) * slab), pltpu.roll(block, (g + 1) * slab, 1), packed)
                turned = jnp.transpose(packed)
                for g in range(4):
                    back_src[p // 2, 4 * i + g] = turned[g * slab : (g + 1) * slab, :]
                return 0

            lax.fori_loop(0, nm // 4, turn_back, 0, unroll=4)

        @pl.when((p == 1) | (p == 3))
        def _():
            back_out(p // 2)

        return 0

    def back_dst(a, many, one):
        return one if isinstance(a, int) and a == STEPS - 1 else many.at[a]

    def back_out(k):
        src, dst = back_dst(k, back_src, last_src), back_dst(k, back_got, last_got)

        def out(i, _):
            to = (m + i) % nm
            send(src.at[to], dst.at[m], b_send.at[k], b_recv.at[k], s, to)
            return 0

        lax.fori_loop(1, nm, out, 0)
        dst[m] = src[m]

    lax.fori_loop(0, 2 * STEPS, apply, 0)

    def line(a, b):
        return jnp.sum(back_src[a] * back_src[b], axis=(0, 1))[None, :]

    pairs = ((0, 0), (0, 1), (1, 1), (0, 2), (1, 2), (2, 2))
    gram = jnp.concatenate([line(a, b) for a, b in pairs] + [jnp.zeros((2, width), F32)], axis=0)
    gram_src[0] = gram
    gram_got[0, m] = gram

    def reduce_mode(k, _):
        to = (m + k) % nm
        send(gram_src.at[0], gram_got.at[0, m], r_send.at[0], r_recv.at[0], s, to)
        return 0

    lax.fori_loop(1, nm, reduce_mode, 0)
    last_src[...] = back_src[STEPS - 1].astype(BF)
    back_out(STEPS - 1)

    arrived(gram_got.at[0, pl.ds(0, nm - 1)], r_recv.at[0])
    gram = jnp.sum(gram_got[0, 0:nm], axis=0)
    gram_src[1] = gram
    gram_got[1, s] = gram

    def reduce_space(k, _):
        to = (s + k) % ns
        send(gram_src.at[1], gram_got.at[1, s], r_send.at[1], r_recv.at[1], to, m)
        return 0

    lax.fori_loop(1, ns, reduce_space, 0)

    for a in range(STEPS):
        arrived(back_dst(a, back_got, last_got).at[pl.ds(0, nm - 1)], b_recv.at[a])

    arrived(gram_got.at[1, pl.ds(0, ns - 1)], r_recv.at[1])
    total = jnp.sum(jnp.sum(gram_got[1, 0:ns], axis=0), axis=1, keepdims=True) * (1.0 / (nodes * ns * nm * width))
    g00, g01, g11, g02, g12, g22 = [total[r : r + 1, :] for r in range(6)]

    def damp(mean_square):
        return step_gain / jnp.sqrt(jnp.maximum(mean_square, 0.0) + 1e-06)

    d0 = damp(g00)
    d1 = damp(g00 - 2.0 * d0 * g01 + d0 * d0 * g11)
    p, q = -(d0 + d1), d0 * d1
    d2 = damp(g00 + p * p * g11 + q * q * g22 + 2.0 * (p * g01 + q * g02 + p * q * g12))
    a0 = d0 + d1 + d2
    a1 = -d0 * d1 - d2 * (d0 + d1)
    a2 = q * d2
    o_ref[...] = a0 * back_got[0] + a1 * back_got[1] + a2 * last_got[...].astype(F32)

    for r in range(3):
        ghosts_sent(r)

    sent(arr_ref.at[:, pl.ds(0, (nm - 1) * slab), :], a_send)
    sent(cv_ref.at[pl.ds(0, nm - 1), pl.ds(0, slots)], c_send)
    for a in range(STEPS):
        sent(back_dst(a, back_src, last_src).at[pl.ds(0, nm - 1)], b_send.at[a])
    sent(gram_got.at[0, pl.ds(0, nm - 1)], r_send.at[0])
    sent(gram_got.at[1, pl.ds(0, ns - 1)], r_send.at[1])


def solution(mesh):
    ns, nm = mesh.shape["space"], mesh.shape["mode"]
    nx = int(round(nm ** 0.5))

    def step(guess, forcing, spatial_diag, spatial_ghost, ghost_rows, chaos_vals, chaos_targets, chaos_count, mean_inverse):
        nodes, width = guess.shape
        ghost = ghost_rows.shape[1]
        blocks, slots = chaos_targets.shape
        modes = blocks * width
        slab = nodes // nm
        lanes = 4 * slab
        vmem = pl.BlockSpec(memory_space=pltpu.VMEM)
        dma = pltpu.SemaphoreType.DMA
        smem, anywhere = pl.BlockSpec(memory_space=pltpu.SMEM), pl.BlockSpec(memory_space=pl.ANY)
        gathered = pl.pallas_call(
            functools.partial(kernel, (ns, nm, nx, slab, ghost, width, slots)),
            out_shape=jax.ShapeDtypeStruct((nm, slab, width), F32),
            in_specs=[anywhere] * 6 + [vmem, smem, anywhere],
            out_specs=vmem,
            scratch_shapes=[
                pltpu.VMEM((nodes, width), F32),
                pltpu.VMEM((nodes, width), F32),
                pltpu.VMEM((nodes, nodes), BF),
                pltpu.VMEM((nodes, 2 * ghost), BF),
                pltpu.VMEM((2, ghost), jnp.int32),
                pltpu.VMEM((2, modes, modes), BF),
                pltpu.VMEM((nm, slots + 1, width, width), BF),
                pltpu.VMEM((blocks, 128), jnp.int32),
                pltpu.SMEM((blocks, 128), jnp.int32),
                pltpu.VMEM((2 * ghost, nodes), BF),
                pltpu.VMEM((7, nodes, width), BF),
                pltpu.VMEM((3, 2 * ghost, 2 * width), BF),
                pltpu.VMEM((3, 2 * ghost, 2 * width), BF),
                pltpu.VMEM((2, nm, lanes, width), BF),
                pltpu.VMEM((2, modes, 2 * lanes), BF),
                pltpu.VMEM((3, modes, lanes), F32),
                pltpu.VMEM((STEPS, nm, slab, width), F32),
                pltpu.VMEM((STEPS - 1, nm, slab, width), F32),
                pltpu.VMEM((nm, slab, width), BF),
                pltpu.VMEM((nm, slab, width), BF),
                pltpu.VMEM((2, 8, width), F32),
                pltpu.VMEM((2, max(nm, ns), 8, width), F32),
                dma((8,)),
                dma((3, 2)), dma((3, 2)),
                dma, dma((2,)),
                dma, dma((2, nm)), dma,
                dma((STEPS,)), dma((STEPS,)),
                dma((2,)), dma((2,)),
            ],
            compiler_params=pltpu.CompilerParams(
                collective_id=0, has_side_effects=True, vmem_limit_bytes=60 * 2**20
            ),
            name="galerkin",
        )(guess, forcing, spatial_diag, spatial_ghost, ghost_rows, chaos_vals, chaos_targets.T, chaos_count, mean_inverse)
        return guess + gathered.reshape(nodes, width)

    space, mode = P("space", "mode"), P("space", None)
    return jax.shard_map(
        step,
        mesh=mesh,
        in_specs=(space, space, mode, mode, mode, P("mode", None, None), P(), P(), P()),
        out_specs=space,
        check_vma=False,
    )
```
